512 devices in a mesh: visit: 64 (over z, y), template: 8 (over x, core).
Axes of the slice: x: 4, y: 4, z: 16, core: 2. Of those that a mesh axis runs over, the one named last changes fastest.
Arguments:
- template: bfloat16 [64, 256, 1152], P('visit', 'template'), may hold values from -5 to 5
- science: bfloat16 [384, 4, 256, 128], P('visit', None, 'template'), may hold values from -27 to 27
- variance: bfloat16 [384, 4, 256, 128], P('visit', None, 'template'), may hold values from 0.5 to 2
- bad_pixels: int32 [384, 4, 256, 128], P('visit', None, 'template'), may hold values 0 or 1
- intersection_patch: int32 [384, 4], P('visit'), may hold values from 0 to 63, as said below
- intersection_block: int32 [384, 4], P('visit'), may hold values from 0 to 7
Outputs:
- significance: float32 [64, 256, 1024], P('visit', 'template')
The draws below stay inside these ranges and needn't reach their ends.
Inputs may be any that keep to these rules, and one draw needn't show every extreme that they name: `intersection_patch`: each visit's 4 patches are different. Among the 6 visits of one index of visit (an aligned block of rows), every patch that is named is named exactly 2 times, and one patch is named 2 times in every such block.
All inputs are finite; a program needn't handle non-finite values. No bound on the sum of `bad_pixels` on one device may be relied on, other than what follows from the above.
Results may differ from the reference program's by a relative error of at most 0.0032.
Values may be sent and summed in bfloat16 or wider, within the bound.
A program may use at most 128 MiB of HBM per device.

```python
import math
import jax
import jax.numpy as jnp
from jax import lax

VIS_DEV = 6
NOV = 4
CB = 128
NBLK = 8
MARGIN = 64
HALF = 10
CAP = 2
VISITS = 384
PATCHES = 64
R = 256
PWIDTH = 1152


def intersection_layout(key):
    folded = jax.random.fold_in(key, 101)
    device_total = VISITS // VIS_DEV
    slot_total = VIS_DEV * NOV
    group_total = slot_total // CAP
    favored = jax.random.randint(jax.random.fold_in(folded, 1), (), 0, PATCHES)

    def arrange(device_key):
        order = jax.random.permutation(jax.random.fold_in(device_key, 2), PATCHES)
        target = jax.random.randint(jax.random.fold_in(device_key, 3), (), 0, group_total)
        position = jnp.argmax(order == favored)
        displaced = order[target]
        order = order.at[position].set(displaced).at[target].set(favored)
        return order[jnp.arange(slot_total) % group_total]
    device_keys = jax.random.split(jax.random.fold_in(folded, 4), device_total)
    return jax.vmap(arrange)(device_keys).reshape(VISITS, NOV).astype(jnp.int32)


def block_layout(key):
    return jax.random.randint(jax.random.fold_in(key, 102), (VISITS, NOV), 0, NBLK).astype(jnp.int32)


def sky_field(key):
    folded = jax.random.fold_in(key, 103)
    sky_values = jnp.clip(jax.random.normal(jax.random.fold_in(folded, 2), (PATCHES, R, PWIDTH), jnp.float32), -5.0, 5.0)
    return sky_values.astype(jnp.bfloat16).astype(jnp.float32)


def draw_template(key, part):
    return sky_field(key).astype(jnp.bfloat16)


def draw_intersection_patch(key, part):
    return intersection_layout(key)


def draw_intersection_block(key, part):
    return block_layout(key)


def draw_science(key, part):
    sky_values = sky_field(key)
    patches = intersection_layout(key)
    columns = block_layout(key)

    def cut_block(patch_id, column_block):
        return lax.dynamic_slice(sky_values, (patch_id, 0, MARGIN + column_block * CB), (1, R, CB))[0]
    region = jax.vmap(jax.vmap(cut_block))(patches, columns)
    folded = jax.random.fold_in(key, 104)
    fraction = jnp.arange(R, dtype=jnp.float32) / max(R - 1, 1)
    row_ramp = 1.0 + 2.0 * fraction
    visit_gain = jnp.exp(jax.random.uniform(jax.random.fold_in(folded, 1), (VISITS, 1, 1, 1), jnp.float32, jnp.log(0.5), jnp.log(1.5)))
    offset = jax.random.uniform(jax.random.fold_in(folded, 2), (VISITS, 1, 1, 1), jnp.float32, -1.0, 1.0)
    noise_part = 0.7 * jnp.clip(jax.random.normal(jax.random.fold_in(folded, 3), (VISITS, NOV, R, CB), jnp.float32), -5.0, 5.0)
    return (visit_gain * row_ramp[None, None, :, None] * region + offset + noise_part).astype(jnp.bfloat16)


def set_ends(drawn, stream_key, least, high):
    longest = drawn.shape.index(max(drawn.shape))
    spots = []
    for shift in (0, 1):
        where = [jax.random.randint(jax.random.fold_in(stream_key, axis), (), 0, length) for axis, length in enumerate(drawn.shape)]
        where[longest] = (where[longest] + shift) % drawn.shape[longest]
        spots.append(tuple(where))
    return drawn.at[spots[0]].set(least).at[spots[1]].set(high)


def steps_of(key, dims, cuts, smallest, largest):
    def one(dim, shards_of):
        draws = jax.random.uniform(jax.random.fold_in(jax.random.fold_in(key, 6), dim), (shards_of,), jnp.float32, smallest / len(cuts), largest / len(cuts))
        return jnp.repeat(jnp.exp(draws), dims[dim] // shards_of).reshape((-1,) + (1,) * (len(dims) - dim - 1))

    factor_of = one(*cuts[0])
    for cut in cuts[1:]:
        factor_of = factor_of * one(*cut)
    return factor_of


def setup_inputs(seed: int = 0) -> dict:
    key_list = jax.random.split(jax.random.key(seed), 7)
    template = draw_template(jax.random.fold_in(key_list[6], 71), 0)
    science = draw_science(jax.random.fold_in(key_list[6], 71), 0)
    variance = jnp.clip(jnp.exp(math.log(2.0) - 1.3862944 * jax.random.uniform(key_list[2], (VISITS, NOV, R, CB), jnp.float32) ** steps_of(key_list[2], (VISITS, NOV, R, CB), ((0, 64), (2, 8)), -0.2, 0.2)), 0.5, 2.0).astype(jnp.bfloat16)
    bad_pixels = set_ends((jax.random.randint(key_list[3], (VISITS, NOV, R, CB), 0, 8) < 1).astype(jnp.int32), jax.random.fold_in(key_list[3], 1), 0, 1)
    intersection_patch = draw_intersection_patch(jax.random.fold_in(key_list[6], 71), 0)
    intersection_block = draw_intersection_block(jax.random.fold_in(key_list[6], 71), 0)
    return dict(template=template, science=science, variance=variance, bad_pixels=bad_pixels, intersection_patch=intersection_patch, intersection_block=intersection_block)


RIDGE = 0.05

def basis_taps():
    spread = jnp.arange(2 * HALF + 1, dtype=jnp.float32)
    scaled = (HALF - spread) / 2.5
    hermite = jnp.stack([jnp.ones(scaled.shape, jnp.float32), 2.0 * scaled, 4.0 * scaled * scaled - 2.0, 8.0 * scaled * scaled * scaled - 12.0 * scaled])
    shaped = hermite * jnp.exp(-0.5 * scaled * scaled)
    shaped = shaped / jnp.sqrt(lax.optimization_barrier(jnp.sum(shaped * shaped, axis=1, keepdims=True)))
    return shaped.astype(jnp.bfloat16)

def solve_normal(system):
    unknowns = system.shape[0]
    rows_index = jnp.arange(unknowns)[:, None, None]
    for column in range(unknowns):
        pivot_row = system[column] / system[column, column][None, :]
        factor = system[:, column, :]
        updated = system - factor[:, None, :] * pivot_row[None, :, :]
        system = jnp.where(rows_index == column, pivot_row[None, :, :], updated)
    return system[:, unknowns, :]

def reference(template, science, variance, bad_pixels, intersection_patch, intersection_block):
    profile = basis_taps().astype(jnp.float32)
    padded = jnp.pad(template, ((0, 0), (HALF, HALF), (0, 0)))
    across = profile[:, None, None, :]
    vertical = profile[:, None, :, None]
    height = R + 2 * HALF
    highest = lax.Precision.HIGHEST

    def visit_step(totals, inputs):
        numerator, denominator = totals
        science_visit, noise_var, masked_bad, patches, columns = inputs

        def cut_block(patch_id, column_block):
            first_column = (column_block * CB + MARGIN - HALF).astype(jnp.int32)
            return lax.dynamic_slice(padded, (patch_id.astype(jnp.int32), jnp.int32(0), first_column), (1, height, CB + 2 * HALF))[0]
        region = jax.vmap(cut_block)(patches, columns).astype(jnp.float32)
        smooth = lax.conv_general_dilated(region[:, None], across, (1, 1), 'VALID', precision=highest)
        smooth = lax.optimization_barrier(smooth.astype(jnp.bfloat16)).astype(jnp.float32)
        basis_images = lax.conv_general_dilated(smooth.reshape(NOV * 4, 1, height, CB), vertical, (1, 1), 'VALID', precision=highest)
        basis_images = basis_images.reshape(NOV, 4, 4, R, CB).transpose(0, 2, 1, 3, 4).reshape(NOV, 16, R, CB)
        basis_images = lax.optimization_barrier(basis_images.astype(jnp.bfloat16)).astype(jnp.float32)
        usable = 1.0 - masked_bad.astype(jnp.float32)
        signal = science_visit.astype(jnp.float32)
        all_columns = jnp.concatenate([basis_images, jnp.ones((NOV, 1, R, CB), jnp.float32), signal[:, None]], axis=1)
        normal = jnp.einsum('jkrc,jlrc->kl', all_columns[:, :17] * usable[:, None], all_columns, precision=highest)
        ridge_term = RIDGE * (normal[16, 16] + 1.0)
        system = normal + ridge_term * jnp.eye(17, 18, dtype=jnp.float32)
        fitted = solve_normal(system[:, :, None])[:, 0]
        modeled = jnp.einsum('jkrc,k->jrc', basis_images, fitted[:16], precision=highest) + fitted[16]
        difference = signal - modeled
        weight = usable / noise_var.astype(jnp.float32)
        sent_numerator = lax.optimization_barrier((weight * difference).astype(jnp.bfloat16)).astype(jnp.float32)
        sent_weight = lax.optimization_barrier(weight.astype(jnp.bfloat16)).astype(jnp.float32)
        target = (patches * NBLK + columns).astype(jnp.int32)
        numerator = numerator.at[target].add(sent_numerator)
        denominator = denominator.at[target].add(sent_weight)
        return ((numerator, denominator), None)
    empty_sums = jnp.zeros((PATCHES * NBLK, R, CB), jnp.float32)
    (numerator, denominator), unused_out = lax.scan(visit_step, (empty_sums, empty_sums), (science, variance, bad_pixels, intersection_patch, intersection_block))
    numerator = numerator.reshape(PATCHES, NBLK, R, CB).transpose(0, 2, 1, 3).reshape(PATCHES, R, NBLK * CB)
    denominator = denominator.reshape(PATCHES, NBLK, R, CB).transpose(0, 2, 1, 3).reshape(PATCHES, R, NBLK * CB)
    return numerator / jnp.sqrt(jnp.maximum(denominator, 1.0))
```

```python
import functools

import jax
import jax.numpy as jnp
import numpy as np
from jax import lax
from jax.experimental import pallas as pl
from jax.experimental.pallas import tpu as pltpu
from jax.sharding import PartitionSpec as P

NBLK = 8
MARGIN = 64
HALF = 10
RIDGE = 0.05
NZ, NY = 16, 4
NDEV = NZ * NY
NTEM = 8
MESH = pl.DeviceIdType.MESH
F32 = jnp.float32
BF16 = jnp.bfloat16


def basis_taps():
    spread = jnp.arange(2 * HALF + 1, dtype=jnp.float32)
    scaled = (HALF - spread) / 2.5
    hermite = jnp.stack(
        [
            jnp.ones(scaled.shape, jnp.float32),
            2.0 * scaled,
            4.0 * scaled * scaled - 2.0,
            8.0 * scaled * scaled * scaled - 12.0 * scaled,
        ]
    )
    shaped = hermite * jnp.exp(-0.5 * scaled * scaled)
    shaped = shaped / jnp.sqrt(jnp.sum(shaped * shaped, axis=1, keepdims=True))
    return shaped.astype(jnp.bfloat16)


def tables():
    profile = np.asarray(basis_taps().astype(jnp.float32))
    across = np.zeros((256, 4, 128), np.float32)
    vertical = np.zeros((4, 32, 64), np.float32)
    for t in range(2 * HALF + 1):
        for c in range(128):
            across[c + t + MARGIN - HALF, :, c] = profile[:, t]
        for r in range(32):
            vertical[:, r, r + t + 16 - HALF] = profile[:, t]
    return across.reshape(256, 512), vertical.reshape(128, 64)


def wrap(value, size):
    return lax.rem(value + size, size)


def gather_kernel(strip, ids, got, got_ids, send_sem, id_send, ay, az, bz, by, iy, iz):
    me = lax.axis_index("visit")
    tem = lax.axis_index("template")
    z, y = lax.div(me, NY), lax.rem(me, NY)

    def at(dz, dy):
        return (wrap(z + dz, NZ) * NY + wrap(y + dy, NY), tem)

    barrier = pltpu.get_barrier_semaphore()
    partners = [at(0, 1), at(0, -1), at(0, 2), at(1, 0), at(-1, 0)]
    for partner in partners:
        pl.semaphore_signal(barrier, inc=1, device_id=partner, device_id_type=MESH)
    pl.semaphore_wait(barrier, len(partners))

    def send(src, dst, sem, recv, target):
        pltpu.make_async_remote_copy(
            src_ref=src, dst_ref=dst, send_sem=sem, recv_sem=recv,
            device_id=target, device_id_type=MESH,
        ).start()

    def arrive(dst, recv):
        pltpu.make_async_copy(dst, dst, recv).wait()

    def slot(zz, yy):
        return wrap(zz, NZ) * NY + wrap(yy, NY)

    def a_ref(zz, yy):
        return got.at[0, slot(zz, yy)]

    def b_ref(zz, yy):
        return got.at[1, slot(zz, yy)]

    for d in (1, 3, 2):
        dy = {1: 1, 2: 2, 3: -1}[d]
        send(ids, got_ids.at[me], id_send, iy.at[d - 1], at(0, dy))
        send(strip.at[0], a_ref(z, y), send_sem, ay.at[d - 1], at(0, dy))
    for k, dz in ((0, 1), (1, -1)):
        send(strip.at[1], b_ref(z, y), send_sem, bz.at[k, 0], at(dz, 0))
        send(strip.at[0], a_ref(z, y), send_sem, az.at[k, 0, 0], at(dz, 0))
    for k, dy in ((0, 1), (1, -1)):
        send(strip.at[1], b_ref(z, y), send_sem, by.at[k, 0], at(0, dy))
    got[0, me] = strip[0]
    got[1, me] = strip[1]
    got_ids[me] = ids[...]
    for d in (1, 3, 2):
        dy = {1: 1, 2: 2, 3: -1}[d]
        arrive(a_ref(z, y - dy), ay.at[d - 1])
        for k, dz in ((0, 1), (1, -1)):
            send(a_ref(z, y - dy), a_ref(z, y - dy), send_sem, az.at[k, 0, d], at(dz, 0))
    for d in (1, 3, 2):
        dy = {1: 1, 2: 2, 3: -1}[d]
        arrive(got_ids.at[slot(z, y - dy)], iy.at[d - 1])
    row = got_ids.at[pl.ds(z * NY, NY)]
    for k, dz in ((0, 1), (1, -1)):
        send(row, row, id_send, iz.at[k, 0], at(dz, 0))

    def relay(source, index):
        k = index % 2
        dy = (1, -1)[k]
        arrive(b_ref(source, y - dy), by.at[k, index])
        send(b_ref(source, y - dy), b_ref(source, y - dy), send_sem, by.at[2, index], at(0, dy))

    half_ring = NZ // 2
    relay(z, 0)
    for s in range(1, half_ring + 1):
        for k, dz in ((0, 1), (1, -1)):
            last = s == half_ring
            if last and k == 1:
                continue
            source = z - dz * s
            index = 2 * s - 1 + k
            arrive(b_ref(source, y), bz.at[k, s - 1])
            if s < half_ring - k:
                send(b_ref(source, y), b_ref(source, y), send_sem, bz.at[k, s], at(dz, 0))
            for q, dy in ((0, 1), (1, -1)):
                send(b_ref(source, y), b_ref(source, y), send_sem, by.at[q, index], at(0, dy))
        for d in (0, 1, 3, 2):
            for k, dz in ((0, 1), (1, -1)):
                dy = {0: 0, 1: 1, 2: 2, 3: -1}[d]
                source = z - dz * s
                if s == half_ring and k != (d >= 2):
                    continue
                arrive(a_ref(source, y - dy), az.at[k, s - 1, d])
                if s < half_ring - 1 or (s == half_ring - 1 and k == (d >= 2)):
                    ref = a_ref(source, y - dy)
                    send(ref, ref, send_sem, az.at[k, s, d], at(dz, 0))
        for k, dz in ((0, 1), (1, -1)):
            if s == half_ring and k == 1:
                continue
            source = z - dz * s
            ref = got_ids.at[pl.ds(wrap(source, NZ) * NY, NY)]
            arrive(ref, iz.at[k, s - 1])
            if s < half_ring - k:
                send(ref, ref, id_send, iz.at[k, s], at(dz, 0))
        for k, dz in ((0, 1), (1, -1)):
            if s == half_ring and k == 1:
                continue
            relay(z - dz * s, 2 * s - 1 + k)
    for index in range(NZ):
        s = (index + 1) // 2
        source = z if index == 0 else (z - s if index % 2 == 1 else z + s)
        k = index % 2
        dy = (1, -1)[k]
        arrive(b_ref(source, y + dy), by.at[1 - k, index])
        arrive(b_ref(source, y + 2), by.at[2, index])
    sent = got.at[:, pl.ds(0, NDEV - 1)]
    arrive(sent, send_sem)
    arrive(got_ids.at[pl.ds(0, NDEV - 1)], id_send)


def gather(strip, ids):
    vmem = pl.BlockSpec(memory_space=pltpu.VMEM)
    dma = pltpu.SemaphoreType.DMA
    return pl.pallas_call(
        gather_kernel,
        out_shape=(
            jax.ShapeDtypeStruct((2, NDEV, 16, strip.shape[-1]), BF16),
            jax.ShapeDtypeStruct((NDEV, 1, 128), jnp.int32),
        ),
        in_specs=[vmem, vmem],
        out_specs=(vmem, vmem),
        scratch_shapes=[
            dma, dma, dma((3,)), dma((2, 8, 4)), dma((2, 8)), dma((3, NZ)), dma((3,)), dma((2, 8)),
        ],
        compiler_params=pltpu.CompilerParams(collective_id=0, has_side_effects=True),
    )(strip, ids)


def cut_kernel(patch, block, got, cut, sem):
    for k in range(24):
        first = pl.multiple_of(block[k] * 128, 128)
        for h in range(2):
            pltpu.make_async_copy(
                got.at[h, patch[k], :, pl.ds(first, 256)], cut.at[h, k], sem
            ).start()
    pltpu.make_async_copy(cut, cut, sem).wait()


def cut_blocks(patch, block, got):
    smem = pl.BlockSpec(memory_space=pltpu.SMEM)
    return pl.pallas_call(
        cut_kernel,
        out_shape=jax.ShapeDtypeStruct((2, 24, 16, 256), BF16),
        in_specs=[smem, smem, pl.BlockSpec(memory_space=pl.ANY)],
        out_specs=pl.BlockSpec(memory_space=pltpu.VMEM),
        scratch_shapes=[pltpu.SemaphoreType.DMA],
    )(patch, block, got)


def fit_kernel(
    core, science, variance, bad, across, vertical, payload,
    rim, smooth, images, part, parts, rows, coef, packed, halo_send, halo_recv, sum_send, sum_recv,
):
    me = lax.axis_index("visit")
    tem = lax.axis_index("template")
    visits = science.shape[0]

    barrier = pltpu.get_barrier_semaphore()
    for d in range(1, NTEM):
        pl.semaphore_signal(
            barrier, inc=1, device_id=(me, wrap(tem + d, NTEM)), device_id_type=MESH
        )
    pl.semaphore_wait(barrier, NTEM - 1)

    def halo(source, dest, step, k):
        return pltpu.make_async_remote_copy(
            src_ref=core.at[source], dst_ref=rim.at[dest],
            send_sem=halo_send.at[k], recv_sem=halo_recv.at[k],
            device_id=(me, wrap(tem + step, NTEM)), device_id_type=MESH,
        )

    down, up = halo(1, 0, 1, 0), halo(0, 1, -1, 1)

    @pl.when(tem < NTEM - 1)
    def _():
        down.start()

    @pl.when(tem > 0)
    def _():
        up.start()

    def smear(piece, source):
        result = jnp.dot(
            source.reshape(24 * 16, 256), across[...], preferred_element_type=F32
        )
        smooth[:, piece * 16 : piece * 16 + 16, :] = result.astype(BF16).reshape(24, 16, 512)

    smear(1, core[0])
    smear(2, core[1])

    @pl.when(tem == 0)
    def _():
        rim[0] = jnp.zeros((24, 16, 256), BF16)

    @pl.when(tem == NTEM - 1)
    def _():
        rim[1] = jnp.zeros((24, 16, 256), BF16)

    @pl.when(tem > 0)
    def _():
        down.wait_recv()

    smear(0, rim[0])

    @pl.when(tem < NTEM - 1)
    def _():
        up.wait_recv()

    smear(3, rim[1])

    part[...] = jnp.zeros((24, 128), F32)
    row_id = lax.broadcasted_iota(jnp.int32, (544, 576), 0) & 31
    lane_id = lax.broadcasted_iota(jnp.int32, (544, 576), 1) & 31
    same_row = row_id == lane_id
    pick_row = lax.broadcasted_iota(jnp.int32, (576, 128), 0) >> 5
    pick_lane = lax.broadcasted_iota(jnp.int32, (576, 128), 1)

    def gram(v, carry):
        for j in range(4):
            image = jnp.dot(
                vertical[...], smooth[v * 4 + j], preferred_element_type=F32
            ).astype(BF16)
            for a in range(4):
                images[v, a * 128 : a * 128 + 128, j * 128 : j * 128 + 128] = image[
                    :, a * 128 : a * 128 + 128
                ]
        usable = jnp.concatenate(
            [(1 - bad[v, j]).astype(F32).astype(BF16) for j in range(4)], axis=1
        )
        signal = jnp.concatenate([science[v, j] for j in range(4)], axis=1)
        left = images[v]
        right = jnp.concatenate(
            [left * jnp.concatenate([usable] * 16, axis=0), usable, usable * signal], axis=0
        )
        left = jnp.concatenate([left, usable], axis=0)
        full = lax.dot_general(
            left, right, (((1,), (1,)), ((), ())), preferred_element_type=F32
        )
        full = jnp.where(same_row, full, 0.0)
        sums = jnp.sum(full.reshape(17, 32, 576), axis=1)
        pick = (pick_lane == pick_row + v * 20).astype(F32)
        part[0:17, :] += jnp.dot(
            sums, pick, preferred_element_type=F32, precision=lax.Precision.HIGHEST
        )
        return carry

    lax.fori_loop(0, visits, gram, 0)

    def share(d):
        return pltpu.make_async_remote_copy(
            src_ref=part, dst_ref=parts.at[tem],
            send_sem=sum_send, recv_sem=sum_recv,
            device_id=(me, wrap(tem + d, NTEM)), device_id_type=MESH,
        )

    for d in range(1, NTEM):
        share(d).start()
    parts[tem] = part[...]
    seven = parts.at[pl.ds(0, NTEM - 1)]
    pltpu.make_async_copy(seven, seven, sum_recv).wait()
    total = parts[0]
    for d in range(1, NTEM):
        total = total + parts[d]

    rows[...] = jnp.zeros((192, 128), F32)
    for v in range(visits):
        moved = total if v == 0 else pltpu.roll(total, 128 - 20 * v, 1)
        rows[pl.ds(v, 24, stride=8), :] = moved
    lane = lax.broadcasted_iota(jnp.int32, (8, 128), 1)
    system = [rows[k * 8 : k * 8 + 8, :] for k in range(17)]
    ridge = RIDGE * (system[16][:, 16:17] + 1.0)
    system = [jnp.where(lane == k, system[k] + ridge, system[k]) for k in range(17)]
    for c in range(17):
        pivot = system[c] / system[c][:, c : c + 1]
        system = [
            pivot if k == c else system[k] - system[k][:, c : c + 1] * pivot for k in range(17)
        ]
    for k in range(17):
        coef[k] = jnp.broadcast_to(system[k][:, 17:18], (8, 128))

    low = lax.broadcasted_iota(jnp.int32, (32, 128), 1) < 64

    def differ(v, carry):
        factors = [
            jnp.broadcast_to(coef[k, pl.ds(v, 1), :], (32, 128)) for k in range(17)
        ]
        for j in range(4):
            model = factors[16]
            for k in range(16):
                model = model + factors[k] * images[
                    v, k * 32 : k * 32 + 32, j * 128 : j * 128 + 128
                ].astype(F32)
            difference = science[v, j].astype(F32) - model
            weight = (1 - bad[v, j]).astype(F32) / variance[v, j].astype(F32)
            number = weight * difference
            first = jnp.where(low, number, pltpu.roll(weight, 64, 1))
            second = jnp.where(low, pltpu.roll(number, 64, 1), weight)
            packed[pl.ds(v * 4 + j, 32, stride=24), :] = first
            packed[pl.ds(768 + v * 4 + j, 32, stride=24), :] = second
        return carry

    lax.fori_loop(0, visits, differ, 0)
    payload[...] = packed[...].reshape(NDEV, 3, 8, 128).astype(BF16)

    @pl.when(tem < NTEM - 1)
    def _():
        down.wait_send()

    @pl.when(tem > 0)
    def _():
        up.wait_send()

    pltpu.make_async_copy(seven, seven, sum_send).wait()


def fit(core, science, variance, bad, across, vertical):
    vmem = pl.BlockSpec(memory_space=pltpu.VMEM)
    dma = pltpu.SemaphoreType.DMA
    return pl.pallas_call(
        fit_kernel,
        out_shape=jax.ShapeDtypeStruct((NDEV, 3, 8, 128), BF16),
        in_specs=[vmem] * 6,
        out_specs=vmem,
        scratch_shapes=[
            pltpu.VMEM((2, 24, 16, 256), BF16),
            pltpu.VMEM((24, 64, 512), BF16),
            pltpu.VMEM((6, 512, 512), BF16),
            pltpu.VMEM((24, 128), F32),
            pltpu.VMEM((NTEM, 24, 128), F32),
            pltpu.VMEM((192, 128), F32),
            pltpu.VMEM((17, 8, 128), F32),
            pltpu.VMEM((1536, 128), F32),
            dma((2,)), dma((2,)), dma, dma,
        ],
        compiler_params=pltpu.CompilerParams(collective_id=1, has_side_effects=True),
    )(core, science, variance, bad, across, vertical)


def return_kernel(target, payload, out, inbox, result, final, send1, recv1, send2, recv2):
    me = lax.axis_index("visit")
    tem = lax.axis_index("template")

    def peer(s):
        return lax.rem(me + s, NDEV)

    barrier = pltpu.get_barrier_semaphore()

    def greet(s, carry):
        pl.semaphore_signal(barrier, inc=1, device_id=(peer(s), tem), device_id_type=MESH)
        return carry

    lax.fori_loop(1, NDEV, greet, 0)
    pl.semaphore_wait(barrier, NDEV - 1)

    def push(s, carry):
        pltpu.make_async_remote_copy(
            src_ref=payload.at[peer(s)], dst_ref=inbox.at[me], send_sem=send1, recv_sem=recv1,
            device_id=(peer(s), tem), device_id_type=MESH,
        ).start()
        return carry

    lax.fori_loop(1, NDEV, push, 0)
    inbox[me] = payload[me]
    choose = (
        lax.broadcasted_iota(jnp.int32, (512, 1536), 0) == target[...]
    ).astype(F32).astype(BF16)
    others = inbox.at[pl.ds(0, NDEV - 1)]
    pltpu.make_async_copy(others, others, recv1).wait()
    values = inbox[...].astype(F32).reshape(1536, 128).astype(BF16)
    sums = jnp.dot(choose, values, preferred_element_type=F32)
    weight = pltpu.roll(sums, 64, 1)
    ratio = sums / jnp.sqrt(jnp.maximum(weight, 1.0))
    low = lax.broadcasted_iota(jnp.int32, (256, 128), 1) < 64
    both = jnp.where(low, ratio[0:256], pltpu.roll(ratio[256:512], 64, 1))
    result[...] = both.reshape(NDEV, 4, 128)

    def give(s, carry):
        pltpu.make_async_remote_copy(
            src_ref=result.at[peer(s)], dst_ref=final.at[me], send_sem=send2, recv_sem=recv2,
            device_id=(peer(s), tem), device_id_type=MESH,
        ).start()
        return carry

    lax.fori_loop(1, NDEV, give, 0)
    final[me] = result[me]
    rest = final.at[pl.ds(0, NDEV - 1)]
    pltpu.make_async_copy(rest, rest, recv2).wait()
    whole = final[...]
    low = lax.broadcasted_iota(jnp.int32, (32, 128), 1) < 64
    for m in range(4):
        left, right = whole[0:32, m, :], whole[32:64, m, :]
        even = jnp.where(low, left, pltpu.roll(right, 64, 1))
        odd = jnp.where(low, pltpu.roll(left, 64, 1), right)
        out[:, m * 256 : m * 256 + 128] = even
        out[:, m * 256 + 128 : m * 256 + 256] = odd
    pltpu.make_async_copy(others, others, send1).wait()
    pltpu.make_async_copy(rest, rest, send2).wait()


def give_back(target, payload):
    vmem = pl.BlockSpec(memory_space=pltpu.VMEM)
    dma = pltpu.SemaphoreType.DMA
    return pl.pallas_call(
        return_kernel,
        out_shape=jax.ShapeDtypeStruct((32, 1024), F32),
        in_specs=[vmem, vmem],
        out_specs=vmem,
        scratch_shapes=[
            pltpu.VMEM((NDEV, 3, 8, 128), BF16),
            pltpu.VMEM((NDEV, 4, 128), F32),
            pltpu.VMEM((NDEV, 4, 128), F32),
            dma, dma, dma, dma,
        ],
        compiler_params=pltpu.CompilerParams(collective_id=2, has_side_effects=True),
    )(target, payload)


def body(across, vertical, template, science, variance, bad_pixels, patch, block):
    patch = patch.reshape(24)
    block = block.reshape(24)
    target = (block % 2) * 256 + patch * 4 + block // 2
    ids = jnp.pad(target, (0, 104)).reshape(1, 128)
    got, got_ids = gather(template.reshape(2, 16, template.shape[-1]), ids)
    payload = fit(cut_blocks(patch, block, got), science, variance, bad_pixels, across, vertical)
    targets = got_ids[:, 0, :24].reshape(1, 1536)
    return give_back(targets, payload)[None]


def solution(mesh):
    with jax.ensure_compile_time_eval():
        across, vertical = tables()
    across = jnp.asarray(across).astype(BF16)
    vertical = jnp.asarray(vertical).astype(BF16)
    return jax.shard_map(
        functools.partial(body, across, vertical),
        mesh=mesh,
        in_specs=(
            P("visit", "template", None),
            P("visit", None, "template", None),
            P("visit", None, "template", None),
            P("visit", None, "template", None),
            P("visit", None),
            P("visit", None),
        ),
        out_specs=P("visit", "template", None),
        check_vma=False,
    )
```

```python
import functools

import jax
import jax.numpy as jnp
import numpy as np
from jax import lax
from jax.experimental import pallas as pl
from jax.experimental.pallas import tpu as pltpu
from jax.sharding import PartitionSpec as P

NBLK = 8
MARGIN = 64
HALF = 10
RIDGE = 0.05
NZ, NY = 16, 4
NDEV = NZ * NY
NTEM = 8
MESH = pl.DeviceIdType.MESH
F32 = jnp.float32
BF16 = jnp.bfloat16


def basis_taps():
    spread = jnp.arange(2 * HALF + 1, dtype=jnp.float32)
    scaled = (HALF - spread) / 2.5
    hermite = jnp.stack(
        [
            jnp.ones(scaled.shape, jnp.float32),
            2.0 * scaled,
            4.0 * scaled * scaled - 2.0,
            8.0 * scaled * scaled * scaled - 12.0 * scaled,
        ]
    )
    shaped = hermite * jnp.exp(-0.5 * scaled * scaled)
    shaped = shaped / jnp.sqrt(jnp.sum(shaped * shaped, axis=1, keepdims=True))
    return shaped.astype(jnp.bfloat16)


def tables():
    profile = np.asarray(basis_taps().astype(jnp.float32))
    across = np.zeros((256, 4, 128), np.float32)
    vertical = np.zeros((4, 32, 64), np.float32)
    for t in range(2 * HALF + 1):
        for c in range(128):
            across[c + t + MARGIN - HALF, :, c] = profile[:, t]
        for r in range(32):
            vertical[:, r, r + t + 16 - HALF] = profile[:, t]
    return across.reshape(256, 512), vertical.reshape(128, 64)


def wrap(value, size):
    return lax.rem(value + size, size)


TILES = 9
LEAD = 7
SLOTS = 24
HALFWAY = (1, -1)
Y_STEP = {0: 0, 1: 1, 2: 2, 3: -1}


def kernel(
    patch, block, strip, science, variance, bad, across, vertical, out,
    stage, got, packed, early, late, early_in, late_in, core, rim, smooth, images,
    part, parts, rows, coef, choose, spread, result, final,
    local_sem, send_sem, ay, az, bz, by, halo_send, halo_recv, sum_send, sum_recv,
    early_send, early_recv, late_send, late_recv, final_send, final_recv,
):
    me = lax.axis_index("visit")
    tem = lax.axis_index("template")
    z, y = lax.div(me, NY), lax.rem(me, NY)
    visits = science.shape[0]

    def at(dz, dy):
        return (wrap(z + dz, NZ) * NY + wrap(y + dy, NY), tem)

    def beside(step):
        return (me, wrap(tem + step, NTEM))

    def send(src, dst, sem, recv, target):
        copy = pltpu.make_async_remote_copy(
            src_ref=src, dst_ref=dst, send_sem=sem, recv_sem=recv,
            device_id=target, device_id_type=MESH,
        )
        copy.start()
        return copy

    def arrive(ref, sem):
        pltpu.make_async_copy(ref, ref, sem).wait()

    barrier = pltpu.get_barrier_semaphore()
    partners = [at(0, 1), at(0, -1), at(0, 2), at(1, 0), at(-1, 0)]
    partners += [beside(d) for d in range(1, NTEM)]
    for partner in partners:
        pl.semaphore_signal(barrier, inc=1, device_id=partner, device_id_type=MESH)

    for h in range(2):
        for c in range(TILES):
            pltpu.make_async_copy(
                strip.at[pl.ds(16 * h, 16), pl.ds(128 * c, 128)],
                stage.at[h * TILES + c],
                local_sem,
            ).start()

    low = lax.broadcasted_iota(jnp.int32, (32, 128), 1) < 64
    for v in range(visits):
        for j in range(4):
            weight = (1 - bad[v, j]).astype(F32) / variance[v, j].astype(F32)
            code = (block[v, j] & 1) * 256 + patch[v, j] * 4 + (block[v, j] >> 1) - 256
            code = jnp.full((32, 128), code, jnp.int32).astype(F32)
            packed[pl.ds(v * 4 + j, 32, stride=SLOTS), :] = jnp.where(
                low, code, pltpu.roll(weight, 64, 1)
            )
            packed[pl.ds(768 + v * 4 + j, 32, stride=SLOTS), :] = jnp.where(low, code, weight)
    early[...] = packed[...].reshape(NDEV, 3, 8, 128).astype(BF16)

    arrive(stage, local_sem)
    pl.semaphore_wait(barrier, len(partners))

    def slot(zz, yy):
        return wrap(zz, NZ) * NY + wrap(yy, NY)

    def a_ref(zz, yy):
        return got.at[slot(zz, yy), pl.ds(0, LEAD)]

    def b_ref(zz, yy):
        return got.at[slot(zz, yy), pl.ds(LEAD, 2 * TILES - LEAD)]

    a_own, b_own = stage.at[pl.ds(0, LEAD)], stage.at[pl.ds(LEAD, 2 * TILES - LEAD)]
    for d in (1, 3, 2):
        send(a_own, a_ref(z, y), send_sem, ay.at[d - 1], at(0, Y_STEP[d]))
    for k, dz in enumerate(HALFWAY):
        send(b_own, b_ref(z, y), send_sem, bz.at[k, 0], at(dz, 0))
        send(a_own, a_ref(z, y), send_sem, az.at[k, 0, 0], at(dz, 0))
    for k, dy in enumerate(HALFWAY):
        send(b_own, b_ref(z, y), send_sem, by.at[k, 0], at(0, dy))
    got[me] = stage[...]
    for d in (1, 3, 2):
        ref = a_ref(z, y - Y_STEP[d])
        arrive(ref, ay.at[d - 1])
        for k, dz in enumerate(HALFWAY):
            send(ref, ref, send_sem, az.at[k, 0, d], at(dz, 0))

    def relay(source, index):
        k = index % 2
        dy = HALFWAY[k]
        ref = b_ref(source, y - dy)
        arrive(ref, by.at[k, index])
        send(ref, ref, send_sem, by.at[2, index], at(0, dy))

    ring = NZ // 2
    for s in range(1, ring + 1):
        for k, dz in enumerate(HALFWAY):
            if s == ring and k == 1:
                continue
            ref = b_ref(z - dz * s, y)
            arrive(ref, bz.at[k, s - 1])
            if s < ring - k:
                send(ref, ref, send_sem, bz.at[k, s], at(dz, 0))
            for q, dy in enumerate(HALFWAY):
                send(ref, ref, send_sem, by.at[q, 2 * s - 1 + k], at(0, dy))
        for d in (0, 1, 3, 2):
            for k, dz in enumerate(HALFWAY):
                if s == ring and k != (d >= 2):
                    continue
                ref = a_ref(z - dz * s, y - Y_STEP[d])
                arrive(ref, az.at[k, s - 1, d])
                if s < ring - 1 or (s == ring - 1 and k == (d >= 2)):
                    send(ref, ref, send_sem, az.at[k, s, d], at(dz, 0))
        if s == 1:
            relay(z, 0)
        else:
            for k, dz in enumerate(HALFWAY):
                relay(z - dz * (s - 1), 2 * (s - 1) - 1 + k)
    relay(z - ring, NZ - 1)
    for index in range(NZ):
        s = (index + 1) // 2
        source = z - s if index % 2 == 1 else z + s
        k = index % 2
        arrive(b_ref(source, y + HALFWAY[k]), by.at[1 - k, index])
        arrive(b_ref(source, y + 2), by.at[2, index])

    def peer(s):
        return lax.rem(me + s, NDEV)

    def push(source, dest, sem, recv):
        def one(s, carry):
            send(source.at[peer(s)], dest.at[me], sem, recv, (peer(s), tem))
            return carry

        lax.fori_loop(1, NDEV, one, 0)

    push(early, early_in, early_send, early_recv)

    for v in range(visits):
        for j in range(4):
            p, b = patch[v, j], block[v, j]
            for h in range(2):
                core[h, v * 4 + j, :, 0:128] = got[p, h * TILES + b]
                core[h, v * 4 + j, :, 128:256] = got[p, h * TILES + b + 1]

    def halo(source, dest, step, k):
        return pltpu.make_async_remote_copy(
            src_ref=core.at[source], dst_ref=rim.at[dest],
            send_sem=halo_send.at[k], recv_sem=halo_recv.at[k],
            device_id=beside(step), device_id_type=MESH,
        )

    down, up = halo(1, 0, 1, 0), halo(0, 1, -1, 1)

    @pl.when(tem < NTEM - 1)
    def _():
        down.start()

    @pl.when(tem > 0)
    def _():
        up.start()

    def smear(piece, source):
        image = jnp.dot(
            source.reshape(SLOTS * 16, 256), across[...], preferred_element_type=F32
        )
        smooth[:, piece * 16 : piece * 16 + 16, :] = image.astype(BF16).reshape(SLOTS, 16, 512)

    early_in[me] = early[me]
    smear(1, core[0])
    smear(2, core[1])

    @pl.when(tem == 0)
    def _():
        rim[0] = jnp.zeros((SLOTS, 16, 256), BF16)

    @pl.when(tem == NTEM - 1)
    def _():
        rim[1] = jnp.zeros((SLOTS, 16, 256), BF16)

    @pl.when(tem > 0)
    def _():
        down.wait_recv()

    smear(0, rim[0])

    @pl.when(tem < NTEM - 1)
    def _():
        up.wait_recv()

    smear(3, rim[1])
    part[...] = jnp.zeros((24, 128), F32)
    row_id = lax.broadcasted_iota(jnp.int32, (544, 576), 0) & 31
    lane_id = lax.broadcasted_iota(jnp.int32, (544, 576), 1) & 31
    same_row = row_id == lane_id
    pick_row = lax.broadcasted_iota(jnp.int32, (576, 128), 0) >> 5
    pick_lane = lax.broadcasted_iota(jnp.int32, (576, 128), 1)

    def gram(v, carry):
        for j in range(4):
            image = jnp.dot(
                vertical[...], smooth[v * 4 + j], preferred_element_type=F32
            ).astype(BF16)
            for a in range(4):
                images[v, a * 128 : a * 128 + 128, j * 128 : j * 128 + 128] = image[
                    :, a * 128 : a * 128 + 128
                ]
        usable = jnp.concatenate(
            [(1 - bad[v, j]).astype(F32).astype(BF16) for j in range(4)], axis=1
        )
        signal = jnp.concatenate([science[v, j] for j in range(4)], axis=1)
        left = images[v]
        right = jnp.concatenate(
            [left * jnp.concatenate([usable] * 16, axis=0), usable, usable * signal], axis=0
        )
        left = jnp.concatenate([left, usable], axis=0)
        full = lax.dot_general(
            left, right, (((1,), (1,)), ((), ())), preferred_element_type=F32
        )
        full = jnp.where(same_row, full, 0.0)
        sums = jnp.sum(full.reshape(17, 32, 576), axis=1)
        pick = (pick_lane == pick_row + v * 20).astype(F32)
        part[0:17, :] += jnp.dot(
            sums, pick, preferred_element_type=F32, precision=lax.Precision.HIGHEST
        )
        return carry

    lax.fori_loop(0, visits, gram, 0)

    for d in range(1, NTEM):
        send(part, parts.at[tem], sum_send, sum_recv, beside(d))
    parts[tem] = part[...]
    seven = parts.at[pl.ds(0, NTEM - 1)]
    arrive(seven, sum_recv)
    total = parts[0]
    for d in range(1, NTEM):
        total = total + parts[d]

    rows[...] = jnp.zeros((192, 128), F32)
    for v in range(visits):
        moved = total if v == 0 else pltpu.roll(total, 128 - 20 * v, 1)
        rows[pl.ds(v, 24, stride=8), :] = moved
    lane = lax.broadcasted_iota(jnp.int32, (8, 128), 1)
    system = [rows[k * 8 : k * 8 + 8, :] for k in range(17)]
    ridge = RIDGE * (system[16][:, 16:17] + 1.0)
    system = [jnp.where(lane == k, system[k] + ridge, system[k]) for k in range(17)]
    for c in range(17):
        pivot = system[c] / system[c][:, c : c + 1]
        system = [
            pivot if k == c else system[k] - system[k][:, c : c + 1] * pivot for k in range(17)
        ]
    for k in range(17):
        coef[k] = jnp.broadcast_to(system[k][:, 17:18], (8, 128))

    def differ(v, carry):
        for j in range(4):
            numbers = []
            for w in (v, v + 3):
                model = jnp.broadcast_to(coef[16, pl.ds(w, 1), :], (32, 128))
                for k in range(16):
                    factor = jnp.broadcast_to(coef[k, pl.ds(w, 1), :], (32, 128))
                    image = images[w, k * 32 : k * 32 + 32, j * 128 : j * 128 + 128]
                    model = model + factor * image.astype(F32)
                weight = (1 - bad[w, j]).astype(F32) / variance[w, j].astype(F32)
                numbers.append(weight * (science[w, j].astype(F32) - model))
            here, there = numbers
            packed[pl.ds(v * 4 + j, 32, stride=12), :] = jnp.where(
                low, here, pltpu.roll(there, 64, 1)
            )
            packed[pl.ds(384 + v * 4 + j, 32, stride=12), :] = jnp.where(
                low, pltpu.roll(here, 64, 1), there
            )
        return carry

    lax.fori_loop(0, visits // 2, differ, 0)
    for k in range(NDEV):
        late[k] = packed[k * 12 : k * 12 + 12, :].astype(BF16)
    push(late, late_in, late_send, late_recv)
    late_in[me] = late[me]

    arrive(early_in.at[pl.ds(0, NDEV - 1)], early_recv)
    values = early_in[...].astype(F32).reshape(NDEV * SLOTS, 128)
    lanes = lax.broadcasted_iota(jnp.int32, (NDEV * SLOTS, 128), 1)
    code = jnp.where(lanes < 64, values, pltpu.roll(values, 64, 1))
    place = lanes.astype(F32)
    for q in range(4):
        choose[:, q * 128 : q * 128 + 128] = jnp.where(
            code == place + (q * 128.0 - 256.0), 1.0, 0.0
        ).astype(BF16)
    inner = (((0,), (0,)), ((), ()))
    denominator = lax.dot_general(
        values.astype(BF16), choose[...], inner, preferred_element_type=F32
    )[64:128]
    scale = jnp.sqrt(jnp.maximum(denominator, 1.0))

    arrive(late_in.at[pl.ds(0, NDEV - 1)], late_recv)
    for k in range(NDEV):
        value = late_in[k].astype(F32)
        spread[k, 0:12, :] = value
        spread[k, 12:24, :] = pltpu.roll(value, 64, 1)
    numerator = lax.dot_general(
        spread[...].reshape(NDEV * SLOTS, 128).astype(BF16), choose[...], inner,
        preferred_element_type=F32,
    )[0:64]
    ratio = numerator / scale
    both = jnp.concatenate([ratio[:, 0:256], ratio[:, 256:512]], axis=0).T
    result[...] = both.reshape(NDEV, 4, 128)
    push(result, final, final_send, final_recv)
    final[me] = result[me]
    arrive(final.at[pl.ds(0, NDEV - 1)], final_recv)
    whole = final[...]
    for m in range(4):
        left, right = whole[0:32, m, :], whole[32:64, m, :]
        out[:, m * 256 : m * 256 + 128] = jnp.where(low, left, pltpu.roll(right, 64, 1))
        out[:, m * 256 + 128 : m * 256 + 256] = jnp.where(low, pltpu.roll(left, 64, 1), right)

    arrive(got.at[pl.ds(0, NDEV - 1)], send_sem)
    arrive(seven, sum_send)
    arrive(early.at[pl.ds(0, NDEV - 1)], early_send)
    arrive(late.at[pl.ds(0, NDEV - 1)], late_send)
    arrive(result.at[pl.ds(0, NDEV - 1)], final_send)

    @pl.when(tem < NTEM - 1)
    def _():
        down.wait_send()

    @pl.when(tem > 0)
    def _():
        up.wait_send()


def body(across, vertical, template, science, variance, bad_pixels, patch, block):
    vmem = pl.BlockSpec(memory_space=pltpu.VMEM)
    smem = pl.BlockSpec(memory_space=pltpu.SMEM)
    anywhere = pl.BlockSpec(memory_space=pl.ANY)
    dma = pltpu.SemaphoreType.DMA
    return pl.pallas_call(
        kernel,
        out_shape=jax.ShapeDtypeStruct((32, 1024), F32),
        in_specs=[smem, smem, anywhere] + [vmem] * 5,
        out_specs=vmem,
        scratch_shapes=[
            pltpu.VMEM((18, 16, 128), BF16),
            pltpu.VMEM((NDEV, 18, 16, 128), BF16),
            pltpu.VMEM((1536, 128), F32),
            pltpu.VMEM((NDEV, 3, 8, 128), BF16),
            pltpu.VMEM((NDEV, 12, 128), BF16),
            pltpu.VMEM((NDEV, 3, 8, 128), BF16),
            pltpu.VMEM((NDEV, 12, 128), BF16),
            pltpu.VMEM((2, SLOTS, 16, 256), BF16),
            pltpu.VMEM((2, SLOTS, 16, 256), BF16),
            pltpu.VMEM((SLOTS, 64, 512), BF16),
            pltpu.VMEM((6, 512, 512), BF16),
            pltpu.VMEM((24, 128), F32),
            pltpu.VMEM((NTEM, 24, 128), F32),
            pltpu.VMEM((192, 128), F32),
            pltpu.VMEM((17, 8, 128), F32),
            pltpu.VMEM((1536, 512), BF16),
            pltpu.VMEM((NDEV, SLOTS, 128), F32),
            pltpu.VMEM((NDEV, 4, 128), F32),
            pltpu.VMEM((NDEV, 4, 128), F32),
            dma, dma, dma((3,)), dma((2, 8, 4)), dma((2, 8)), dma((3, NZ)),
            dma((2,)), dma((2,)), dma, dma, dma, dma, dma, dma, dma, dma,
        ],
        compiler_params=pltpu.CompilerParams(collective_id=0, has_side_effects=True),
    )(patch, block, template[0], science, variance, bad_pixels, across, vertical)[None]


def solution(mesh):
    with jax.ensure_compile_time_eval():
        across, vertical = tables()
    across = jnp.asarray(across).astype(BF16)
    vertical = jnp.asarray(vertical).astype(BF16)
    return jax.shard_map(
        functools.partial(body, across, vertical),
        mesh=mesh,
        in_specs=(
            P("visit", "template", None),
            P("visit", None, "template", None),
            P("visit", None, "template", None),
            P("visit", None, "template", None),
            P("visit", None),
            P("visit", None),
        ),
        out_specs=P("visit", "template", None),
        check_vma=False,
    )
```

```python
import functools

import jax
import jax.numpy as jnp
import numpy as np
from jax import lax
from jax.experimental import pallas as pl
from jax.experimental.pallas import tpu as pltpu
from jax.sharding import PartitionSpec as P

NBLK = 8
MARGIN = 64
HALF = 10
RIDGE = 0.05
NZ, NY = 16, 4
NDEV = NZ * NY
NTEM = 8
MESH = pl.DeviceIdType.MESH
F32 = jnp.float32
BF16 = jnp.bfloat16


def basis_taps():
    spread = jnp.arange(2 * HALF + 1, dtype=jnp.float32)
    scaled = (HALF - spread) / 2.5
    hermite = jnp.stack(
        [
            jnp.ones(scaled.shape, jnp.float32),
            2.0 * scaled,
            4.0 * scaled * scaled - 2.0,
            8.0 * scaled * scaled * scaled - 12.0 * scaled,
        ]
    )
    shaped = hermite * jnp.exp(-0.5 * scaled * scaled)
    shaped = shaped / jnp.sqrt(jnp.sum(shaped * shaped, axis=1, keepdims=True))
    return shaped.astype(jnp.bfloat16)


def tables():
    profile = np.asarray(basis_taps().astype(jnp.float32))
    across = np.zeros((256, 4, 128), np.float32)
    vertical = np.zeros((4, 32, 64), np.float32)
    for t in range(2 * HALF + 1):
        for c in range(128):
            across[c + t + MARGIN - HALF, :, c] = profile[:, t]
        for r in range(32):
            vertical[:, r, r + t + 16 - HALF] = profile[:, t]
    return across.reshape(256, 512), vertical.reshape(128, 64)


def wrap(value, size):
    return lax.rem(value + size, size)


TILES = 9
LEAD = 8
SLOTS = 24
HALFWAY = (1, -1)
Y_STEP = {0: 0, 1: 1, 2: 2, 3: -1}


def kernel(
    patch, block, strip, science, variance, bad, across, vertical, out,
    stage, got, packed, early, late, early_in, late_in, core, rim, smooth, images,
    sums, part, parts, rows, coef, codes, column, choose, spread, result, final,
    local_sem, send_sem, ay, az, bz, by, halo_send, halo_recv, sum_send, sum_recv,
    early_send, early_recv, late_send, late_recv, final_send, final_recv,
):
    me = lax.axis_index("visit")
    tem = lax.axis_index("template")
    z, y = lax.div(me, NY), lax.rem(me, NY)
    visits = science.shape[0]

    def at(dz, dy):
        return (wrap(z + dz, NZ) * NY + wrap(y + dy, NY), tem)

    def beside(step):
        return (me, wrap(tem + step, NTEM))

    def send(src, dst, sem, recv, target):
        copy = pltpu.make_async_remote_copy(
            src_ref=src, dst_ref=dst, send_sem=sem, recv_sem=recv,
            device_id=target, device_id_type=MESH,
        )
        copy.start()
        return copy

    def arrive(ref, sem):
        pltpu.make_async_copy(ref, ref, sem).wait()

    barrier = pltpu.get_barrier_semaphore()
    partners = [at(0, 1), at(0, -1), at(0, 2), at(1, 0), at(-1, 0)]
    partners += [beside(d) for d in range(1, NTEM)]
    for partner in partners:
        pl.semaphore_signal(barrier, inc=1, device_id=partner, device_id_type=MESH)

    for h in range(2):
        for c in range(TILES):
            pltpu.make_async_copy(
                strip.at[pl.ds(16 * h, 16), pl.ds(128 * c, 128)],
                stage.at[h * TILES + c],
                local_sem,
            ).start()

    low = lax.broadcasted_iota(jnp.int32, (32, 128), 1) < 64
    lane = lax.broadcasted_iota(jnp.int32, (8, 128), 1)

    def weigh(v, j):
        return (1 - bad[v, j]).astype(F32) / variance[v, j].astype(F32)

    def pack(index, here, there, pitch):
        packed[pl.ds(index, 32, stride=pitch), :] = jnp.where(low, here, pltpu.roll(there, 64, 1))
        packed[pl.ds(32 * pitch + index, 32, stride=pitch), :] = jnp.where(
            low, pltpu.roll(here, 64, 1), there
        )

    targets = jnp.zeros((8, 128), F32)
    for v in range(visits):
        for j in range(4):
            code = (block[j, v] & 1) * 256 + patch[j, v] * 4 + (block[j, v] >> 1) - 256
            code = jnp.full((8, 128), code, jnp.int32).astype(F32)
            targets = jnp.where(lane == v * 4 + j, code, targets)
            if v < visits // 2:
                pack(v * 4 + j, weigh(v, j), weigh(v + 3, j), 16)
    packed[pl.ds(12, NDEV, stride=16), :] = jnp.broadcast_to(targets[0:1], (NDEV, 128))
    early[...] = packed[...].reshape(NDEV, 16, 128).astype(BF16)

    arrive(stage, local_sem)
    pl.semaphore_wait(barrier, len(partners))

    def slot(zz, yy):
        return wrap(zz, NZ) * NY + wrap(yy, NY)

    def a_ref(zz, yy):
        return got.at[slot(zz, yy), pl.ds(0, LEAD)]

    def b_ref(zz, yy):
        return got.at[slot(zz, yy), pl.ds(LEAD, 2 * TILES - LEAD)]

    a_own, b_own = stage.at[pl.ds(0, LEAD)], stage.at[pl.ds(LEAD, 2 * TILES - LEAD)]
    for d in (1, 3, 2):
        send(a_own, a_ref(z, y), send_sem, ay.at[d - 1], at(0, Y_STEP[d]))
    for k, dz in enumerate(HALFWAY):
        send(b_own, b_ref(z, y), send_sem, bz.at[k, 0], at(dz, 0))
        send(a_own, a_ref(z, y), send_sem, az.at[k, 0, 0], at(dz, 0))
    for k, dy in enumerate(HALFWAY):
        send(b_own, b_ref(z, y), send_sem, by.at[k, 0], at(0, dy))
    got[me] = stage[...]
    for d in (1, 3, 2):
        ref = a_ref(z, y - Y_STEP[d])
        arrive(ref, ay.at[d - 1])
        for k, dz in enumerate(HALFWAY):
            send(ref, ref, send_sem, az.at[k, 0, d], at(dz, 0))

    def relay(source, index):
        k = index % 2
        dy = HALFWAY[k]
        ref = b_ref(source, y - dy)
        arrive(ref, by.at[k, index])
        send(ref, ref, send_sem, by.at[2, index], at(0, dy))

    ring = NZ // 2
    for s in range(1, ring + 1):
        for k, dz in enumerate(HALFWAY):
            if s == ring and k == 1:
                continue
            ref = b_ref(z - dz * s, y)
            arrive(ref, bz.at[k, s - 1])
            if s < ring - k:
                send(ref, ref, send_sem, bz.at[k, s], at(dz, 0))
            for q, dy in enumerate(HALFWAY):
                send(ref, ref, send_sem, by.at[q, 2 * s - 1 + k], at(0, dy))
        for d in (0, 1, 3, 2):
            for k, dz in enumerate(HALFWAY):
                if s == ring and k != (d >= 2):
                    continue
                ref = a_ref(z - dz * s, y - Y_STEP[d])
                arrive(ref, az.at[k, s - 1, d])
                if s < ring - 1 or (s == ring - 1 and k == (d >= 2)):
                    send(ref, ref, send_sem, az.at[k, s, d], at(dz, 0))
        if s == 1:
            relay(z, 0)
        else:
            for k, dz in enumerate(HALFWAY):
                relay(z - dz * (s - 1), 2 * (s - 1) - 1 + k)
    relay(z - ring, NZ - 1)
    for index in range(NZ):
        s = (index + 1) // 2
        source = z - s if index % 2 == 1 else z + s
        k = index % 2
        arrive(b_ref(source, y + HALFWAY[k]), by.at[1 - k, index])
        arrive(b_ref(source, y + 2), by.at[2, index])

    def peer(s):
        return lax.rem(me + s, NDEV)

    def push(source, dest, sem, recv):
        def one(s):
            send(source.at[peer(s)], dest.at[me], sem, recv, (peer(s), tem))

        def two(m, carry):
            one(NDEV // 2 - m)
            one(NDEV // 2 + m)
            return carry

        one(NDEV // 2)
        lax.fori_loop(1, NDEV // 2, two, 0)

    for v in range(visits):
        for j in range(4):
            p, b = patch[j, v], block[j, v]
            for h in range(2):
                core[h, v * 4 + j, :, 0:128] = got[p, h * TILES + b]
                core[h, v * 4 + j, :, 128:256] = got[p, h * TILES + b + 1]

    def halo(source, dest, step, k):
        return pltpu.make_async_remote_copy(
            src_ref=core.at[source], dst_ref=rim.at[dest],
            send_sem=halo_send.at[k], recv_sem=halo_recv.at[k],
            device_id=beside(step), device_id_type=MESH,
        )

    down, up = halo(1, 0, 1, 0), halo(0, 1, -1, 1)

    @pl.when(tem < NTEM - 1)
    def _():
        down.start()

    @pl.when(tem > 0)
    def _():
        up.start()

    def smear(piece, source):
        image = jnp.dot(
            source.reshape(SLOTS * 16, 256), across[...], preferred_element_type=F32
        )
        smooth[:, piece * 16 : piece * 16 + 16, :] = image.astype(BF16).reshape(SLOTS, 16, 512)

    push(early, early_in, early_send, early_recv)
    early_in[me] = early[me]
    smear(1, core[0])
    smear(2, core[1])

    @pl.when(tem == 0)
    def _():
        rim[0] = jnp.zeros((SLOTS, 16, 256), BF16)

    @pl.when(tem == NTEM - 1)
    def _():
        rim[1] = jnp.zeros((SLOTS, 16, 256), BF16)

    @pl.when(tem > 0)
    def _():
        down.wait_recv()

    smear(0, rim[0])

    @pl.when(tem < NTEM - 1)
    def _():
        up.wait_recv()

    smear(3, rim[1])
    row_id = lax.broadcasted_iota(jnp.int32, (144, 144), 0) & 7
    lane_id = lax.broadcasted_iota(jnp.int32, (144, 144), 1) & 7
    same_row = row_id == lane_id

    def gram(v, carry):
        ones, extra = [None] * 16, [None] * 16
        for j in range(4):
            image = jnp.dot(vertical[...], smooth[v * 4 + j], preferred_element_type=F32)
            usable = (1 - bad[v, j]).astype(F32)
            masked = usable * science[v, j].astype(F32)
            for g in range(4):
                tile = g * 4 + j
                rows_of = slice(g * 8, g * 8 + 8)
                for a in range(4):
                    pieces = [
                        image[b * 32 + g * 8 : b * 32 + g * 8 + 8, a * 128 : a * 128 + 128]
                        for b in range(4)
                    ]
                    images[v, a * 32 : a * 32 + 32, tile * 128 : tile * 128 + 128] = (
                        jnp.concatenate(pieces, axis=0).astype(BF16)
                    )
                some = usable[rows_of]
                ones[tile] = jnp.concatenate([some, some], axis=0).astype(BF16)
                extra[tile] = jnp.concatenate([some, masked[rows_of]], axis=0).astype(BF16)
        ones = jnp.concatenate(ones, axis=1)
        extra = jnp.concatenate(extra, axis=1)
        left = images[v]
        right = jnp.concatenate([left * jnp.concatenate([ones] * 8, axis=0), extra], axis=0)
        left = jnp.concatenate([left, extra], axis=0)
        full = lax.dot_general(
            left, right, (((1,), (1,)), ((), ())), preferred_element_type=F32
        )
        full = jnp.where(same_row, full, 0.0)
        sums[v, 0:18, :] = jnp.sum(full.reshape(18, 8, 144), axis=1)
        sums[v, 18:24, :] = jnp.zeros((6, 144), F32)
        return carry

    lax.fori_loop(0, visits, gram, 0)
    pick_row = lax.broadcasted_iota(jnp.int32, (144, 128), 0) >> 3
    pick_lane = lax.broadcasted_iota(jnp.int32, (144, 128), 1)
    dense = jnp.dot(
        sums[...].reshape(144, 144), (pick_lane == pick_row).astype(F32),
        preferred_element_type=F32, precision=lax.Precision.HIGHEST,
    )
    mine = dense[0:24]
    for v in range(1, visits):
        mine = mine + pltpu.roll(dense[v * 24 : v * 24 + 24], 20 * v, 1)
    part[...] = mine
    for d in range(1, NTEM):
        send(part, parts.at[tem], sum_send, sum_recv, beside(d))
    parts[tem] = part[...]
    seven = parts.at[pl.ds(0, NTEM - 1)]
    arrive(seven, sum_recv)
    total = parts[0]
    for d in range(1, NTEM):
        total = total + parts[d]

    rows[...] = jnp.zeros((192, 128), F32)
    for v in range(visits):
        moved = total if v == 0 else pltpu.roll(total, 128 - 20 * v, 1)
        rows[pl.ds(v, 24, stride=8), :] = moved
    system = [rows[k * 8 : k * 8 + 8, :] for k in range(17)]
    ridge = RIDGE * (system[16][:, 16:17] + 1.0)
    system = [jnp.where(lane == k, system[k] + ridge, system[k]) for k in range(17)]
    for c in range(17):
        pivot = system[c] / system[c][:, c : c + 1]
        system = [
            pivot if k == c else system[k] - system[k][:, c : c + 1] * pivot for k in range(17)
        ]
    for k in range(17):
        coef[k] = jnp.broadcast_to(system[k][:, 17:18], (8, 128))

    def differ(v, carry):
        numbers = []
        for w in (v, v + 3):
            factors = [jnp.broadcast_to(coef[k, pl.ds(w, 1), :], (8, 128)) for k in range(17)]
            for j in range(4):
                models = []
                for g in range(4):
                    tile = g * 4 + j
                    model = factors[16]
                    for a in range(4):
                        image = images[
                            w, a * 32 : a * 32 + 32, tile * 128 : tile * 128 + 128
                        ].astype(F32)
                        for b in range(4):
                            model = model + factors[a * 4 + b] * image[b * 8 : b * 8 + 8]
                    models.append(model)
                model = jnp.concatenate(models, axis=0)
                numbers.append(weigh(w, j) * (science[w, j].astype(F32) - model))
        for j in range(4):
            pack(v * 4 + j, numbers[j], numbers[4 + j], 12)
        return carry

    lax.fori_loop(0, visits // 2, differ, 0)
    for k in range(NDEV):
        late[k] = packed[k * 12 : k * 12 + 12, :].astype(BF16)
    push(late, late_in, late_send, late_recv)
    late_in[me] = late[me]

    arrive(early_in.at[pl.ds(0, NDEV - 1)], early_recv)
    codes[...] = jnp.zeros((128, 128), F32)
    for k in range(NDEV):
        value = early_in[k].astype(F32)
        spread[k, 0:12, :] = value[0:12]
        spread[k, 12:24, :] = pltpu.roll(value[0:12], 64, 1)
        codes[k : k + 1, :] = value[12:13]
    across_codes = codes[...].T
    for k in range(NDEV):
        column[k] = jnp.broadcast_to(across_codes[0:SLOTS, k : k + 1], (SLOTS, 128))
    code = column[...].reshape(NDEV * SLOTS, 128)
    place = lax.broadcasted_iota(jnp.int32, (NDEV * SLOTS, 128), 1).astype(F32)
    for q in range(4):
        choose[:, q * 128 : q * 128 + 128] = jnp.where(
            code == place + (q * 128.0 - 256.0), 1.0, 0.0
        ).astype(BF16)
    inner = (((0,), (0,)), ((), ()))
    denominator = lax.dot_general(
        spread[...].reshape(NDEV * SLOTS, 128).astype(BF16), choose[...], inner,
        preferred_element_type=F32,
    )[0:64]
    scale = jnp.sqrt(jnp.maximum(denominator, 1.0))

    arrive(late_in.at[pl.ds(0, NDEV - 1)], late_recv)
    for k in range(NDEV):
        value = late_in[k].astype(F32)
        spread[k, 0:12, :] = value
        spread[k, 12:24, :] = pltpu.roll(value, 64, 1)
    numerator = lax.dot_general(
        spread[...].reshape(NDEV * SLOTS, 128).astype(BF16), choose[...], inner,
        preferred_element_type=F32,
    )[0:64]
    ratio = numerator / scale
    both = jnp.concatenate([ratio[:, 0:256], ratio[:, 256:512]], axis=0).T
    result[...] = both.reshape(NDEV, 4, 128)
    push(result, final, final_send, final_recv)
    final[me] = result[me]
    arrive(final.at[pl.ds(0, NDEV - 1)], final_recv)
    whole = final[...]
    for m in range(4):
        left, right = whole[0:32, m, :], whole[32:64, m, :]
        out[:, m * 256 : m * 256 + 128] = jnp.where(low, left, pltpu.roll(right, 64, 1))
        out[:, m * 256 + 128 : m * 256 + 256] = jnp.where(low, pltpu.roll(left, 64, 1), right)

    arrive(got.at[pl.ds(0, NDEV - 1)], send_sem)
    arrive(seven, sum_send)
    arrive(early.at[pl.ds(0, NDEV - 1)], early_send)
    arrive(late.at[pl.ds(0, NDEV - 1)], late_send)
    arrive(result.at[pl.ds(0, NDEV - 1)], final_send)

    @pl.when(tem < NTEM - 1)
    def _():
        down.wait_send()

    @pl.when(tem > 0)
    def _():
        up.wait_send()


def body(across, vertical, template, science, variance, bad_pixels, patch, block):
    vmem = pl.BlockSpec(memory_space=pltpu.VMEM)
    smem = pl.BlockSpec(memory_space=pltpu.SMEM)
    anywhere = pl.BlockSpec(memory_space=pl.ANY)
    dma = pltpu.SemaphoreType.DMA
    return pl.pallas_call(
        kernel,
        out_shape=jax.ShapeDtypeStruct((32, 1024), F32),
        in_specs=[smem, smem, anywhere] + [vmem] * 5,
        out_specs=vmem,
        scratch_shapes=[
            pltpu.VMEM((18, 16, 128), BF16),
            pltpu.VMEM((NDEV, 18, 16, 128), BF16),
            pltpu.VMEM((1024, 128), F32),
            pltpu.VMEM((NDEV, 16, 128), BF16),
            pltpu.VMEM((NDEV, 12, 128), BF16),
            pltpu.VMEM((NDEV, 16, 128), BF16),
            pltpu.VMEM((NDEV, 12, 128), BF16),
            pltpu.VMEM((2, SLOTS, 16, 256), BF16),
            pltpu.VMEM((2, SLOTS, 16, 256), BF16),
            pltpu.VMEM((SLOTS, 64, 512), BF16),
            pltpu.VMEM((6, 128, 2048), BF16),
            pltpu.VMEM((6, 24, 144), F32),
            pltpu.VMEM((24, 128), F32),
            pltpu.VMEM((NTEM, 24, 128), F32),
            pltpu.VMEM((192, 128), F32),
            pltpu.VMEM((17, 8, 128), F32),
            pltpu.VMEM((128, 128), F32),
            pltpu.VMEM((NDEV, SLOTS, 128), F32),
            pltpu.VMEM((1536, 512), BF16),
            pltpu.VMEM((NDEV, SLOTS, 128), F32),
            pltpu.VMEM((NDEV, 4, 128), F32),
            pltpu.VMEM((NDEV, 4, 128), F32),
            dma, dma, dma((3,)), dma((2, 8, 4)), dma((2, 8)), dma((3, NZ)),
            dma((2,)), dma((2,)), dma, dma, dma, dma, dma, dma, dma, dma,
        ],
        compiler_params=pltpu.CompilerParams(collective_id=0, has_side_effects=True),
    )(patch.T, block.T, template[0], science, variance, bad_pixels, across, vertical)[None]


def solution(mesh):
    with jax.ensure_compile_time_eval():
        across, vertical = tables()
    across = jnp.asarray(across).astype(BF16)
    vertical = jnp.asarray(vertical).astype(BF16)
    return jax.shard_map(
        functools.partial(body, across, vertical),
        mesh=mesh,
        in_specs=(
            P("visit", "template", None),
            P("visit", None, "template", None),
            P("visit", None, "template", None),
            P("visit", None, "template", None),
            P("visit", None),
            P("visit", None),
        ),
        out_specs=P("visit", "template", None),
        check_vma=False,
    )
```

```python
import functools

import jax
import jax.numpy as jnp
import numpy as np
from jax import lax
from jax.experimental import pallas as pl
from jax.experimental.pallas import tpu as pltpu
from jax.sharding import PartitionSpec as P

NBLK = 8
MARGIN = 64
HALF = 10
RIDGE = 0.05
NZ, NY = 16, 4
NDEV = NZ * NY
NTEM = 8
MESH = pl.DeviceIdType.MESH
F32 = jnp.float32
BF16 = jnp.bfloat16


def basis_taps():
    spread = jnp.arange(2 * HALF + 1, dtype=jnp.float32)
    scaled = (HALF - spread) / 2.5
    hermite = jnp.stack(
        [
            jnp.ones(scaled.shape, jnp.float32),
            2.0 * scaled,
            4.0 * scaled * scaled - 2.0,
            8.0 * scaled * scaled * scaled - 12.0 * scaled,
        ]
    )
    shaped = hermite * jnp.exp(-0.5 * scaled * scaled)
    shaped = shaped / jnp.sqrt(jnp.sum(shaped * shaped, axis=1, keepdims=True))
    return shaped.astype(jnp.bfloat16)


def tables():
    profile = np.asarray(basis_taps().astype(jnp.float32))
    across = np.zeros((256, 4, 128), np.float32)
    vertical = np.zeros((4, 32, 64), np.float32)
    for t in range(2 * HALF + 1):
        for c in range(128):
            across[c + t + MARGIN - HALF, :, c] = profile[:, t]
        for r in range(32):
            vertical[:, r, r + t + 16 - HALF] = profile[:, t]
    return across.reshape(256, 512), vertical.reshape(128, 64)


def wrap(value, size):
    return lax.rem(value + size, size)


TILES = 9
LEAD = 7
SLOTS = 24
HALFWAY = (1, -1)
Y_STEP = {0: 0, 1: 1, 2: 2, 3: -1}


def kernel(
    patch, block, strip, science_in, variance_in, bad_in, across_in, vertical_in, out,
    science, variance, bad, across, vertical,
    stage, got, packed, early, late, early_in, late_in, core, rim, smooth, images,
    sums, part, parts, rows, coef, codes, column, choose, spread, result, final,
    local_sem, input_sem, send_sem, ay, az, bz, by, halo_send, halo_recv, sum_send, sum_recv,
    early_send, early_recv, late_send, late_recv, final_send, final_recv,
):
    me = lax.axis_index("visit")
    tem = lax.axis_index("template")
    z, y = lax.div(me, NY), lax.rem(me, NY)
    visits = science.shape[0]
    inputs = (science, variance, bad, across, vertical)

    def at(dz, dy):
        return (wrap(z + dz, NZ) * NY + wrap(y + dy, NY), tem)

    def beside(step):
        return (me, wrap(tem + step, NTEM))

    def send(src, dst, sem, recv, target):
        copy = pltpu.make_async_remote_copy(
            src_ref=src, dst_ref=dst, send_sem=sem, recv_sem=recv,
            device_id=target, device_id_type=MESH,
        )
        copy.start()
        return copy

    def arrive(ref, sem):
        pltpu.make_async_copy(ref, ref, sem).wait()

    barrier = pltpu.get_barrier_semaphore()
    partners = [at(0, 1), at(0, -1), at(0, 2), at(1, 0), at(-1, 0)]
    partners += [beside(d) for d in range(1, NTEM)]
    for partner in partners:
        pl.semaphore_signal(barrier, inc=1, device_id=partner, device_id_type=MESH)

    for h in range(2):
        for c in range(TILES):
            pltpu.make_async_copy(
                strip.at[pl.ds(16 * h, 16), pl.ds(128 * c, 128)],
                stage.at[h * TILES + c],
                local_sem,
            ).start()

    sources = (science_in, variance_in, bad_in, across_in, vertical_in)
    for k in range(5):
        pltpu.make_async_copy(sources[k], inputs[k], input_sem.at[k]).start()
    arrive(stage, local_sem)
    pl.semaphore_wait(barrier, len(partners))

    def slot(zz, yy):
        return wrap(zz, NZ) * NY + wrap(yy, NY)

    def a_ref(zz, yy):
        return got.at[slot(zz, yy), pl.ds(0, LEAD)]

    def b_ref(zz, yy):
        return got.at[slot(zz, yy), pl.ds(LEAD, 2 * TILES - LEAD)]

    a_own, b_own = stage.at[pl.ds(0, LEAD)], stage.at[pl.ds(LEAD, 2 * TILES - LEAD)]
    for d in (1, 3, 2):
        send(a_own, a_ref(z, y), send_sem, ay.at[d - 1], at(0, Y_STEP[d]))
    for k, dz in enumerate(HALFWAY):
        send(b_own, b_ref(z, y), send_sem, bz.at[k, 0], at(dz, 0))
        send(a_own, a_ref(z, y), send_sem, az.at[k, 0, 0], at(dz, 0))
    for k, dy in enumerate(HALFWAY):
        send(b_own, b_ref(z, y), send_sem, by.at[k, 0], at(0, dy))
    got[me] = stage[...]
    for k in range(5):
        arrive(inputs[k], input_sem.at[k])
    low = lax.broadcasted_iota(jnp.int32, (32, 128), 1) < 64
    lane = lax.broadcasted_iota(jnp.int32, (8, 128), 1)

    def weigh(v, j):
        return (1 - bad[v, j]).astype(F32) / variance[v, j].astype(F32)

    def pack(index, here, there, pitch):
        packed[pl.ds(index, 32, stride=pitch), :] = jnp.where(low, here, pltpu.roll(there, 64, 1))
        packed[pl.ds(32 * pitch + index, 32, stride=pitch), :] = jnp.where(
            low, pltpu.roll(here, 64, 1), there
        )

    targets = jnp.zeros((8, 128), F32)
    for v in range(visits):
        for j in range(4):
            code = (block[j, v] & 1) * 256 + patch[j, v] * 4 + (block[j, v] >> 1) - 256
            code = jnp.full((8, 128), code, jnp.int32).astype(F32)
            targets = jnp.where(lane == v * 4 + j, code, targets)
            if v < visits // 2:
                pack(v * 4 + j, weigh(v, j), weigh(v + 3, j), 16)
    packed[pl.ds(12, NDEV, stride=16), :] = jnp.broadcast_to(targets[0:1], (NDEV, 128))
    early[...] = packed[...].reshape(NDEV, 16, 128).astype(BF16)
    for d in (1, 3, 2):
        ref = a_ref(z, y - Y_STEP[d])
        arrive(ref, ay.at[d - 1])
        for k, dz in enumerate(HALFWAY):
            send(ref, ref, send_sem, az.at[k, 0, d], at(dz, 0))

    def relay(source, index):
        k = index % 2
        dy = HALFWAY[k]
        ref = b_ref(source, y - dy)
        arrive(ref, by.at[k, index])
        send(ref, ref, send_sem, by.at[2, index], at(0, dy))

    ring = NZ // 2

    def z_first(s):
        for k, dz in enumerate(HALFWAY):
            if s == ring and k == 1:
                continue
            ref = b_ref(z - dz * s, y)
            arrive(ref, bz.at[k, s - 1])
            if s < ring - k:
                send(ref, ref, send_sem, bz.at[k, s], at(dz, 0))
            for q, dy in enumerate(HALFWAY):
                send(ref, ref, send_sem, by.at[q, 2 * s - 1 + k], at(0, dy))

    def y_first(s, d):
        for k, dz in enumerate(HALFWAY):
            if s == ring and k != (d >= 2):
                continue
            ref = a_ref(z - dz * s, y - Y_STEP[d])
            arrive(ref, az.at[k, s - 1, d])
            if s < ring - 1 or (s == ring - 1 and k == (d >= 2)):
                send(ref, ref, send_sem, az.at[k, s, d], at(dz, 0))

    def relays(s):
        if s == 0:
            relay(z, 0)
        for k, dz in enumerate(HALFWAY):
            if s > 0 and 2 * s - 1 + k < NZ:
                relay(z - dz * s, 2 * s - 1 + k)

    due = {7 * (s - 1) // 2: s for s in range(1, ring + 1)}
    for index in range(4 * ring):
        if index in due:
            z_first(due[index])
            relays(due[index] - 1)
        if index == 4 * ring - 4:
            relays(ring)
        y_first(index // 4 + 1, (0, 1, 3, 2)[index % 4])
    for index in range(NZ):
        s = (index + 1) // 2
        source = z - s if index % 2 == 1 else z + s
        k = index % 2
        arrive(b_ref(source, y + HALFWAY[k]), by.at[1 - k, index])
        arrive(b_ref(source, y + 2), by.at[2, index])

    def peer(s):
        return lax.rem(me + s, NDEV)

    def push(source, dest, sem, recv):
        def one(s):
            send(source.at[peer(s)], dest.at[me], sem, recv, (peer(s), tem))

        def two(m, carry):
            one(NDEV // 2 - m)
            one(NDEV // 2 + m)
            return carry

        one(NDEV // 2)
        lax.fori_loop(1, NDEV // 2, two, 0)

    for v in range(visits):
        for j in range(4):
            p, b = patch[j, v], block[j, v]
            for h in range(2):
                core[h, v * 4 + j, :, 0:128] = got[p, h * TILES + b]
                core[h, v * 4 + j, :, 128:256] = got[p, h * TILES + b + 1]

    def halo(source, dest, step, k):
        return pltpu.make_async_remote_copy(
            src_ref=core.at[source], dst_ref=rim.at[dest],
            send_sem=halo_send.at[k], recv_sem=halo_recv.at[k],
            device_id=beside(step), device_id_type=MESH,
        )

    down, up = halo(1, 0, 1, 0), halo(0, 1, -1, 1)

    @pl.when(tem < NTEM - 1)
    def _():
        down.start()

    @pl.when(tem > 0)
    def _():
        up.start()

    def smear(piece, source):
        image = jnp.dot(
            source.reshape(SLOTS * 16, 256), across[...], preferred_element_type=F32
        )
        smooth[:, piece * 16 : piece * 16 + 16, :] = image.astype(BF16).reshape(SLOTS, 16, 512)

    push(early, early_in, early_send, early_recv)
    early_in[me] = early[me]
    smear(1, core[0])
    smear(2, core[1])

    @pl.when(tem == 0)
    def _():
        rim[0] = jnp.zeros((SLOTS, 16, 256), BF16)

    @pl.when(tem == NTEM - 1)
    def _():
        rim[1] = jnp.zeros((SLOTS, 16, 256), BF16)

    @pl.when(tem > 0)
    def _():
        down.wait_recv()

    smear(0, rim[0])

    @pl.when(tem < NTEM - 1)
    def _():
        up.wait_recv()

    smear(3, rim[1])
    row_id = lax.broadcasted_iota(jnp.int32, (144, 144), 0) & 7
    lane_id = lax.broadcasted_iota(jnp.int32, (144, 144), 1) & 7
    same_row = row_id == lane_id

    def gram(v, carry):
        ones, extra = [None] * 16, [None] * 16
        for j in range(4):
            image = jnp.dot(vertical[...], smooth[v * 4 + j], preferred_element_type=F32)
            usable = (1 - bad[v, j]).astype(F32)
            masked = usable * science[v, j].astype(F32)
            for g in range(4):
                tile = g * 4 + j
                rows_of = slice(g * 8, g * 8 + 8)
                for a in range(4):
                    pieces = [
                        image[b * 32 + g * 8 : b * 32 + g * 8 + 8, a * 128 : a * 128 + 128]
                        for b in range(4)
                    ]
                    images[v, a * 32 : a * 32 + 32, tile * 128 : tile * 128 + 128] = (
                        jnp.concatenate(pieces, axis=0).astype(BF16)
                    )
                some = usable[rows_of]
                ones[tile] = jnp.concatenate([some, some], axis=0).astype(BF16)
                extra[tile] = jnp.concatenate([some, masked[rows_of]], axis=0).astype(BF16)
        ones = jnp.concatenate(ones, axis=1)
        extra = jnp.concatenate(extra, axis=1)
        left = images[v]
        right = jnp.concatenate([left * jnp.concatenate([ones] * 8, axis=0), extra], axis=0)
        left = jnp.concatenate([left, extra], axis=0)
        full = lax.dot_general(
            left, right, (((1,), (1,)), ((), ())), preferred_element_type=F32
        )
        full = jnp.where(same_row, full, 0.0)
        sums[v, 0:18, :] = jnp.sum(full.reshape(18, 8, 144), axis=1)
        sums[v, 18:24, :] = jnp.zeros((6, 144), F32)
        return carry

    lax.fori_loop(0, visits, gram, 0)
    pick_row = lax.broadcasted_iota(jnp.int32, (144, 128), 0) >> 3
    pick_lane = lax.broadcasted_iota(jnp.int32, (144, 128), 1)
    dense = jnp.dot(
        sums[...].reshape(144, 144), (pick_lane == pick_row).astype(F32),
        preferred_element_type=F32, precision=lax.Precision.HIGHEST,
    )
    mine = dense[0:24]
    for v in range(1, visits):
        mine = mine + pltpu.roll(dense[v * 24 : v * 24 + 24], 20 * v, 1)
    part[...] = mine
    for d in range(1, NTEM):
        send(part, parts.at[tem], sum_send, sum_recv, beside(d))
    parts[tem] = part[...]
    seven = parts.at[pl.ds(0, NTEM - 1)]
    arrive(seven, sum_recv)
    total = parts[0]
    for d in range(1, NTEM):
        total = total + parts[d]

    rows[...] = jnp.zeros((192, 128), F32)
    for v in range(visits):
        moved = total if v == 0 else pltpu.roll(total, 128 - 20 * v, 1)
        rows[pl.ds(v, 24, stride=8), :] = moved
    system = [rows[k * 8 : k * 8 + 8, :] for k in range(17)]
    ridge = RIDGE * (system[16][:, 16:17] + 1.0)
    system = [jnp.where(lane == k, system[k] + ridge, system[k]) for k in range(17)]
    for c in range(17):
        pivot = system[c] / system[c][:, c : c + 1]
        system = [
            pivot if k == c else system[k] - system[k][:, c : c + 1] * pivot for k in range(17)
        ]
    for k in range(17):
        coef[k] = jnp.broadcast_to(system[k][:, 17:18], (8, 128))

    def differ(v, carry):
        numbers = []
        for w in (v, v + 3):
            factors = [jnp.broadcast_to(coef[k, pl.ds(w, 1), :], (8, 128)) for k in range(17)]
            for j in range(4):
                models = []
                for g in range(4):
                    tile = g * 4 + j
                    model = factors[16]
                    for a in range(4):
                        image = images[
                            w, a * 32 : a * 32 + 32, tile * 128 : tile * 128 + 128
                        ].astype(F32)
                        for b in range(4):
                            model = model + factors[a * 4 + b] * image[b * 8 : b * 8 + 8]
                    models.append(model)
                model = jnp.concatenate(models, axis=0)
                numbers.append(weigh(w, j) * (science[w, j].astype(F32) - model))
        for j in range(4):
            pack(v * 4 + j, numbers[j], numbers[4 + j], 12)
        return carry

    lax.fori_loop(0, visits // 2, differ, 0)
    for k in range(NDEV):
        late[k] = packed[k * 12 : k * 12 + 12, :].astype(BF16)
    push(late, late_in, late_send, late_recv)
    late_in[me] = late[me]

    arrive(early_in.at[pl.ds(0, NDEV - 1)], early_recv)
    codes[...] = jnp.zeros((128, 128), F32)
    for k in range(NDEV):
        value = early_in[k].astype(F32)
        spread[k, 0:12, :] = value[0:12]
        spread[k, 12:24, :] = pltpu.roll(value[0:12], 64, 1)
        codes[k : k + 1, :] = value[12:13]
    across_codes = codes[...].T
    for k in range(NDEV):
        column[k] = jnp.broadcast_to(across_codes[0:SLOTS, k : k + 1], (SLOTS, 128))
    code = column[...].reshape(NDEV * SLOTS, 128)
    place = lax.broadcasted_iota(jnp.int32, (NDEV * SLOTS, 128), 1).astype(F32)
    for q in range(4):
        choose[:, q * 128 : q * 128 + 128] = jnp.where(
            code == place + (q * 128.0 - 256.0), 1.0, 0.0
        ).astype(BF16)
    inner = (((0,), (0,)), ((), ()))
    denominator = lax.dot_general(
        spread[...].reshape(NDEV * SLOTS, 128).astype(BF16), choose[...], inner,
        preferred_element_type=F32,
    )[0:64]
    scale = jnp.sqrt(jnp.maximum(denominator, 1.0))

    arrive(late_in.at[pl.ds(0, NDEV - 1)], late_recv)
    for k in range(NDEV):
        value = late_in[k].astype(F32)
        spread[k, 0:12, :] = value
        spread[k, 12:24, :] = pltpu.roll(value, 64, 1)
    numerator = lax.dot_general(
        spread[...].reshape(NDEV * SLOTS, 128).astype(BF16), choose[...], inner,
        preferred_element_type=F32,
    )[0:64]
    ratio = numerator / scale
    both = jnp.concatenate([ratio[:, 0:256], ratio[:, 256:512]], axis=0).T
    result[...] = both.reshape(NDEV, 4, 128)
    push(result, final, final_send, final_recv)
    final[me] = result[me]
    arrive(final.at[pl.ds(0, NDEV - 1)], final_recv)
    whole = final[...]
    for m in range(4):
        left, right = whole[0:32, m, :], whole[32:64, m, :]
        out[:, m * 256 : m * 256 + 128] = jnp.where(low, left, pltpu.roll(right, 64, 1))
        out[:, m * 256 + 128 : m * 256 + 256] = jnp.where(low, pltpu.roll(left, 64, 1), right)

    arrive(got.at[pl.ds(0, NDEV - 1)], send_sem)
    arrive(seven, sum_send)
    arrive(early.at[pl.ds(0, NDEV - 1)], early_send)
    arrive(late.at[pl.ds(0, NDEV - 1)], late_send)
    arrive(result.at[pl.ds(0, NDEV - 1)], final_send)

    @pl.when(tem < NTEM - 1)
    def _():
        down.wait_send()

    @pl.when(tem > 0)
    def _():
        up.wait_send()


def body(across, vertical, template, science, variance, bad_pixels, patch, block):
    vmem = pl.BlockSpec(memory_space=pltpu.VMEM)
    smem = pl.BlockSpec(memory_space=pltpu.SMEM)
    anywhere = pl.BlockSpec(memory_space=pl.ANY)
    dma = pltpu.SemaphoreType.DMA
    return pl.pallas_call(
        kernel,
        out_shape=jax.ShapeDtypeStruct((32, 1024), F32),
        in_specs=[smem, smem] + [anywhere] * 6,
        out_specs=vmem,
        scratch_shapes=[
            pltpu.VMEM(science.shape, BF16),
            pltpu.VMEM(variance.shape, BF16),
            pltpu.VMEM(bad_pixels.shape, jnp.int32),
            pltpu.VMEM(across.shape, BF16),
            pltpu.VMEM(vertical.shape, BF16),
            pltpu.VMEM((18, 16, 128), BF16),
            pltpu.VMEM((NDEV, 18, 16, 128), BF16),
            pltpu.VMEM((1024, 128), F32),
            pltpu.VMEM((NDEV, 16, 128), BF16),
            pltpu.VMEM((NDEV, 12, 128), BF16),
            pltpu.VMEM((NDEV, 16, 128), BF16),
            pltpu.VMEM((NDEV, 12, 128), BF16),
            pltpu.VMEM((2, SLOTS, 16, 256), BF16),
            pltpu.VMEM((2, SLOTS, 16, 256), BF16),
            pltpu.VMEM((SLOTS, 64, 512), BF16),
            pltpu.VMEM((6, 128, 2048), BF16),
            pltpu.VMEM((6, 24, 144), F32),
            pltpu.VMEM((24, 128), F32),
            pltpu.VMEM((NTEM, 24, 128), F32),
            pltpu.VMEM((192, 128), F32),
            pltpu.VMEM((17, 8, 128), F32),
            pltpu.VMEM((128, 128), F32),
            pltpu.VMEM((NDEV, SLOTS, 128), F32),
            pltpu.VMEM((1536, 512), BF16),
            pltpu.VMEM((NDEV, SLOTS, 128), F32),
            pltpu.VMEM((NDEV, 4, 128), F32),
            pltpu.VMEM((NDEV, 4, 128), F32),
            dma, dma((5,)), dma, dma((3,)), dma((2, 8, 4)), dma((2, 8)), dma((3, NZ)),
            dma((2,)), dma((2,)), dma, dma, dma, dma, dma, dma, dma, dma,
        ],
        compiler_params=pltpu.CompilerParams(collective_id=0, has_side_effects=True),
    )(patch.T, block.T, template[0], science, variance, bad_pixels, across, vertical)[None]


def solution(mesh):
    with jax.ensure_compile_time_eval():
        across, vertical = tables()
    across = jnp.asarray(across).astype(BF16)
    vertical = jnp.asarray(vertical).astype(BF16)
    return jax.shard_map(
        functools.partial(body, across, vertical),
        mesh=mesh,
        in_specs=(
            P("visit", "template", None),
            P("visit", None, "template", None),
            P("visit", None, "template", None),
            P("visit", None, "template", None),
            P("visit", None),
            P("visit", None),
        ),
        out_specs=P("visit", "template", None),
        check_vma=False,
    )
```

```python
import functools

import jax
import jax.numpy as jnp
import numpy as np
from jax import lax
from jax.experimental import pallas as pl
from jax.experimental.pallas import tpu as pltpu
from jax.sharding import PartitionSpec as P

NBLK = 8
MARGIN = 64
HALF = 10
RIDGE = 0.05
NZ, NY = 16, 4
NDEV = NZ * NY
NTEM = 8
MESH = pl.DeviceIdType.MESH
F32 = jnp.float32
BF16 = jnp.bfloat16


def basis_taps():
    spread = jnp.arange(2 * HALF + 1, dtype=jnp.float32)
    scaled = (HALF - spread) / 2.5
    hermite = jnp.stack(
        [
            jnp.ones(scaled.shape, jnp.float32),
            2.0 * scaled,
            4.0 * scaled * scaled - 2.0,
            8.0 * scaled * scaled * scaled - 12.0 * scaled,
        ]
    )
    shaped = hermite * jnp.exp(-0.5 * scaled * scaled)
    shaped = shaped / jnp.sqrt(jnp.sum(shaped * shaped, axis=1, keepdims=True))
    return shaped.astype(jnp.bfloat16)


def tables():
    profile = np.asarray(basis_taps().astype(jnp.float32))
    across = np.zeros((256, 4, 128), np.float32)
    vertical = np.zeros((4, 32, 64), np.float32)
    for t in range(2 * HALF + 1):
        for c in range(128):
            across[c + t + MARGIN - HALF, :, c] = profile[:, t]
        for r in range(32):
            vertical[:, r, r + t + 16 - HALF] = profile[:, t]
    return across.reshape(256, 512), vertical.reshape(128, 64)


def wrap(value, size):
    return lax.rem(value + size, size)


TILES = 9
LEAD = 9
SLOTS = 24
HALFWAY = (1, -1)
Y_STEP = {0: 0, 1: 1, 2: 2, 3: -1}


def kernel(
    patch, block, strip, science_in, variance_in, bad_in, across_in, vertical_in, out,
    science, variance, bad, across, vertical,
    stage, got, packed, early, late, early_in, late_in, core, rim, smooth, images,
    sums, part, parts, rows, coef, codes, column, choose, spread, result, final,
    local_sem, input_sem, send_sem, ay, az, bz, by, halo_send, halo_recv, sum_send, sum_recv,
    early_send, early_recv, late_send, late_recv, final_send, final_recv,
):
    me = lax.axis_index("visit")
    tem = lax.axis_index("template")
    z, y = lax.div(me, NY), lax.rem(me, NY)
    visits = science.shape[0]
    inputs = (science, variance, bad, across, vertical)

    def at(dz, dy):
        return (wrap(z + dz, NZ) * NY + wrap(y + dy, NY), tem)

    def beside(step):
        return (me, wrap(tem + step, NTEM))

    def send(src, dst, sem, recv, target):
        copy = pltpu.make_async_remote_copy(
            src_ref=src, dst_ref=dst, send_sem=sem, recv_sem=recv,
            device_id=target, device_id_type=MESH,
        )
        copy.start()
        return copy

    def arrive(ref, sem):
        pltpu.make_async_copy(ref, ref, sem).wait()

    barrier = pltpu.get_barrier_semaphore()
    partners = [at(0, 1), at(0, -1), at(0, 2), at(1, 0), at(-1, 0)]
    partners += [beside(d) for d in range(1, NTEM)]
    for partner in partners:
        pl.semaphore_signal(barrier, inc=1, device_id=partner, device_id_type=MESH)

    for h in range(2):
        for c in range(TILES):
            pltpu.make_async_copy(
                strip.at[pl.ds(16 * h, 16), pl.ds(128 * c, 128)],
                stage.at[h * TILES + c],
                local_sem,
            ).start()

    sources = (science_in, variance_in, bad_in, across_in, vertical_in)
    for k in range(5):
        pltpu.make_async_copy(sources[k], inputs[k], input_sem.at[k]).start()
    arrive(stage, local_sem)
    pl.semaphore_wait(barrier, len(partners))

    def slot(zz, yy):
        return wrap(zz, NZ) * NY + wrap(yy, NY)

    def a_ref(zz, yy):
        return got.at[slot(zz, yy), pl.ds(0, LEAD)]

    def b_ref(zz, yy):
        return got.at[slot(zz, yy), pl.ds(LEAD, 2 * TILES - LEAD)]

    a_own, b_own = stage.at[pl.ds(0, LEAD)], stage.at[pl.ds(LEAD, 2 * TILES - LEAD)]
    for d in (1, 3, 2):
        send(a_own, a_ref(z, y), send_sem, ay.at[d - 1], at(0, Y_STEP[d]))
    for k, dz in enumerate(HALFWAY):
        send(b_own, b_ref(z, y), send_sem, bz.at[k, 0], at(dz, 0))
        send(a_own, a_ref(z, y), send_sem, az.at[k, 0, 0], at(dz, 0))
    for k, dy in enumerate(HALFWAY):
        send(b_own, b_ref(z, y), send_sem, by.at[k, 0], at(0, dy))
    got[me] = stage[...]
    for k in range(5):
        arrive(inputs[k], input_sem.at[k])
    low = lax.broadcasted_iota(jnp.int32, (32, 128), 1) < 64
    lane = lax.broadcasted_iota(jnp.int32, (8, 128), 1)

    def weigh(v, j):
        return (1 - bad[v, j]).astype(F32) / variance[v, j].astype(F32)

    def pack(index, here, there, pitch):
        packed[pl.ds(index, 32, stride=pitch), :] = jnp.where(low, here, pltpu.roll(there, 64, 1))
        packed[pl.ds(32 * pitch + index, 32, stride=pitch), :] = jnp.where(
            low, pltpu.roll(here, 64, 1), there
        )

    targets = jnp.zeros((8, 128), F32)
    for v in range(visits):
        for j in range(4):
            code = (block[j, v] & 1) * 256 + patch[j, v] * 4 + (block[j, v] >> 1) - 256
            code = jnp.full((8, 128), code, jnp.int32).astype(F32)
            targets = jnp.where(lane == v * 4 + j, code, targets)
            if v < visits // 2:
                pack(v * 4 + j, weigh(v, j), weigh(v + 3, j), 16)
    packed[pl.ds(12, NDEV, stride=16), :] = jnp.broadcast_to(targets[0:1], (NDEV, 128))
    early[...] = packed[...].reshape(NDEV, 16, 128).astype(BF16)
    for d in (1, 3, 2):
        ref = a_ref(z, y - Y_STEP[d])
        arrive(ref, ay.at[d - 1])
        for k, dz in enumerate(HALFWAY):
            send(ref, ref, send_sem, az.at[k, 0, d], at(dz, 0))

    def relay(source, index):
        k = index % 2
        dy = HALFWAY[k]
        ref = b_ref(source, y - dy)
        arrive(ref, by.at[k, index])
        send(ref, ref, send_sem, by.at[2, index], at(0, dy))

    ring = NZ // 2

    def z_first(s):
        for k, dz in enumerate(HALFWAY):
            if s == ring and k == 1:
                continue
            ref = b_ref(z - dz * s, y)
            arrive(ref, bz.at[k, s - 1])
            if s < ring - k:
                send(ref, ref, send_sem, bz.at[k, s], at(dz, 0))
            for q, dy in enumerate(HALFWAY):
                send(ref, ref, send_sem, by.at[q, 2 * s - 1 + k], at(0, dy))

    def y_first(s, d):
        for k, dz in enumerate(HALFWAY):
            if s == ring and k != (d >= 2):
                continue
            ref = a_ref(z - dz * s, y - Y_STEP[d])
            arrive(ref, az.at[k, s - 1, d])
            if s < ring - 1 or (s == ring - 1 and k == (d >= 2)):
                send(ref, ref, send_sem, az.at[k, s, d], at(dz, 0))

    def relays(s):
        if s == 0:
            relay(z, 0)
        for k, dz in enumerate(HALFWAY):
            if s > 0 and 2 * s - 1 + k < NZ:
                relay(z - dz * s, 2 * s - 1 + k)

    due = {7 * (s - 1) // 2: s for s in range(1, ring + 1)}
    for index in range(4 * ring):
        if index in due:
            z_first(due[index])
            relays(due[index] - 1)
        if index == 4 * ring - 4:
            relays(ring)
        y_first(index // 4 + 1, (0, 1, 3, 2)[index % 4])
    for index in range(NZ):
        s = (index + 1) // 2
        source = z - s if index % 2 == 1 else z + s
        k = index % 2
        arrive(b_ref(source, y + HALFWAY[k]), by.at[1 - k, index])
        arrive(b_ref(source, y + 2), by.at[2, index])

    def peer(s):
        return lax.rem(me + s, NDEV)

    def push(source, dest, sem, recv):
        def one(s):
            send(source.at[peer(s)], dest.at[me], sem, recv, (peer(s), tem))

        def two(m, carry):
            one(NDEV // 2 - m)
            one(NDEV // 2 + m)
            return carry

        one(NDEV // 2)
        lax.fori_loop(1, NDEV // 2, two, 0)

    def halo(half, source, dest, step, k):
        return pltpu.make_async_remote_copy(
            src_ref=core.at[half, source], dst_ref=rim.at[half, dest],
            send_sem=halo_send.at[half, k], recv_sem=halo_recv.at[half, k],
            device_id=beside(step), device_id_type=MESH,
        )

    downs = [halo(half, 1, 0, 1, 0) for half in range(2)]
    ups = [halo(half, 0, 1, -1, 1) for half in range(2)]
    for half in range(2):
        for v in range(3):
            for j in range(4):
                p, b = patch[j, half * 3 + v], block[j, half * 3 + v]
                for h in range(2):
                    core[half, h, v * 4 + j, :, 0:128] = got[p, h * TILES + b]
                    core[half, h, v * 4 + j, :, 128:256] = got[p, h * TILES + b + 1]

        @pl.when(tem < NTEM - 1)
        def _():
            downs[half].start()

        @pl.when(tem > 0)
        def _():
            ups[half].start()

    def smear(half, piece, source):
        image = jnp.dot(
            source.reshape(12 * 16, 256), across[...], preferred_element_type=F32
        )
        smooth[half * 12 : half * 12 + 12, piece * 16 : piece * 16 + 16, :] = image.astype(
            BF16
        ).reshape(12, 16, 512)

    push(early, early_in, early_send, early_recv)
    early_in[me] = early[me]
    for half in range(2):
        smear(half, 1, core[half, 0])
        smear(half, 2, core[half, 1])

    @pl.when(tem == 0)
    def _():
        rim[:, 0] = jnp.zeros((2, 12, 16, 256), BF16)

    @pl.when(tem == NTEM - 1)
    def _():
        rim[:, 1] = jnp.zeros((2, 12, 16, 256), BF16)

    row_id = lax.broadcasted_iota(jnp.int32, (144, 144), 0) & 7
    lane_id = lax.broadcasted_iota(jnp.int32, (144, 144), 1) & 7
    same_row = row_id == lane_id

    def gram(v, carry):
        ones, extra = [None] * 16, [None] * 16
        for j in range(4):
            image = jnp.dot(vertical[...], smooth[v * 4 + j], preferred_element_type=F32)
            usable = (1 - bad[v, j]).astype(F32)
            masked = usable * science[v, j].astype(F32)
            for g in range(4):
                tile = g * 4 + j
                rows_of = slice(g * 8, g * 8 + 8)
                for a in range(4):
                    pieces = [
                        image[b * 32 + g * 8 : b * 32 + g * 8 + 8, a * 128 : a * 128 + 128]
                        for b in range(4)
                    ]
                    images[v, a * 32 : a * 32 + 32, tile * 128 : tile * 128 + 128] = (
                        jnp.concatenate(pieces, axis=0).astype(BF16)
                    )
                some = usable[rows_of]
                ones[tile] = jnp.concatenate([some, some], axis=0).astype(BF16)
                extra[tile] = jnp.concatenate([some, masked[rows_of]], axis=0).astype(BF16)
        ones = jnp.concatenate(ones, axis=1)
        extra = jnp.concatenate(extra, axis=1)
        left = images[v]
        right = jnp.concatenate([left * jnp.concatenate([ones] * 8, axis=0), extra], axis=0)
        left = jnp.concatenate([left, extra], axis=0)
        full = lax.dot_general(
            left, right, (((1,), (1,)), ((), ())), preferred_element_type=F32
        )
        full = jnp.where(same_row, full, 0.0)
        sums[v, 0:18, :] = jnp.sum(full.reshape(18, 8, 144), axis=1)
        sums[v, 18:24, :] = jnp.zeros((6, 144), F32)
        return carry

    for half in range(2):

        @pl.when(tem > 0)
        def _():
            downs[half].wait_recv()

        @pl.when(tem < NTEM - 1)
        def _():
            ups[half].wait_recv()

        smear(half, 0, rim[half, 0])
        smear(half, 3, rim[half, 1])
        lax.fori_loop(half * 3, half * 3 + 3, gram, 0)
    pick_row = lax.broadcasted_iota(jnp.int32, (144, 128), 0) >> 3
    pick_lane = lax.broadcasted_iota(jnp.int32, (144, 128), 1)
    dense = jnp.dot(
        sums[...].reshape(144, 144), (pick_lane == pick_row).astype(F32),
        preferred_element_type=F32, precision=lax.Precision.HIGHEST,
    )
    mine = dense[0:24]
    for v in range(1, visits):
        mine = mine + pltpu.roll(dense[v * 24 : v * 24 + 24], 20 * v, 1)
    part[...] = mine
    for d in range(1, NTEM):
        send(part, parts.at[tem], sum_send, sum_recv, beside(d))
    parts[tem] = part[...]
    seven = parts.at[pl.ds(0, NTEM - 1)]
    arrive(seven, sum_recv)
    total = parts[0]
    for d in range(1, NTEM):
        total = total + parts[d]

    rows[...] = jnp.zeros((192, 128), F32)
    for v in range(visits):
        moved = total if v == 0 else pltpu.roll(total, 128 - 20 * v, 1)
        rows[pl.ds(v, 24, stride=8), :] = moved
    system = [rows[k * 8 : k * 8 + 8, :] for k in range(17)]
    ridge = RIDGE * (system[16][:, 16:17] + 1.0)
    system = [jnp.where(lane == k, system[k] + ridge, system[k]) for k in range(17)]
    for c in range(17):
        pivot = system[c] / system[c][:, c : c + 1]
        system = [
            pivot if k == c else system[k] - system[k][:, c : c + 1] * pivot for k in range(17)
        ]
    for k in range(17):
        coef[k] = jnp.broadcast_to(system[k][:, 17:18], (8, 128))

    def differ(v, carry):
        numbers = []
        for w in (v, v + 3):
            factors = [jnp.broadcast_to(coef[k, pl.ds(w, 1), :], (8, 128)) for k in range(17)]
            for j in range(4):
                models = []
                for g in range(4):
                    tile = g * 4 + j
                    model = factors[16]
                    for a in range(4):
                        image = images[
                            w, a * 32 : a * 32 + 32, tile * 128 : tile * 128 + 128
                        ].astype(F32)
                        for b in range(4):
                            model = model + factors[a * 4 + b] * image[b * 8 : b * 8 + 8]
                    models.append(model)
                model = jnp.concatenate(models, axis=0)
                numbers.append(weigh(w, j) * (science[w, j].astype(F32) - model))
        for j in range(4):
            pack(v * 4 + j, numbers[j], numbers[4 + j], 12)
        return carry

    lax.fori_loop(0, visits // 2, differ, 0)
    for k in range(NDEV):
        late[k] = packed[k * 12 : k * 12 + 12, :].astype(BF16)
    push(late, late_in, late_send, late_recv)
    late_in[me] = late[me]

    arrive(early_in.at[pl.ds(0, NDEV - 1)], early_recv)
    codes[...] = jnp.zeros((128, 128), F32)
    for k in range(NDEV):
        value = early_in[k].astype(F32)
        spread[k, 0:12, :] = value[0:12]
        spread[k, 12:24, :] = pltpu.roll(value[0:12], 64, 1)
        codes[k : k + 1, :] = value[12:13]
    across_codes = codes[...].T
    for k in range(NDEV):
        column[k] = jnp.broadcast_to(across_codes[0:SLOTS, k : k + 1], (SLOTS, 128))
    code = column[...].reshape(NDEV * SLOTS, 128)
    place = lax.broadcasted_iota(jnp.int32, (NDEV * SLOTS, 128), 1).astype(F32)
    for q in range(4):
        choose[:, q * 128 : q * 128 + 128] = jnp.where(
            code == place + (q * 128.0 - 256.0), 1.0, 0.0
        ).astype(BF16)
    inner = (((0,), (0,)), ((), ()))
    denominator = lax.dot_general(
        spread[...].reshape(NDEV * SLOTS, 128).astype(BF16), choose[...], inner,
        preferred_element_type=F32,
    )[0:64]
    scale = jnp.sqrt(jnp.maximum(denominator, 1.0))

    arrive(late_in.at[pl.ds(0, NDEV - 1)], late_recv)
    for k in range(NDEV):
        value = late_in[k].astype(F32)
        spread[k, 0:12, :] = value
        spread[k, 12:24, :] = pltpu.roll(value, 64, 1)
    numerator = lax.dot_general(
        spread[...].reshape(NDEV * SLOTS, 128).astype(BF16), choose[...], inner,
        preferred_element_type=F32,
    )[0:64]
    ratio = numerator / scale
    both = jnp.concatenate([ratio[:, 0:256], ratio[:, 256:512]], axis=0).T
    result[...] = both.reshape(NDEV, 4, 128).astype(BF16)
    push(result, final, final_send, final_recv)
    final[me] = result[me]
    arrive(final.at[pl.ds(0, NDEV - 1)], final_recv)
    whole = final[...].astype(F32)
    for m in range(4):
        left, right = whole[0:32, m, :], whole[32:64, m, :]
        out[:, m * 256 : m * 256 + 128] = jnp.where(low, left, pltpu.roll(right, 64, 1))
        out[:, m * 256 + 128 : m * 256 + 256] = jnp.where(low, pltpu.roll(left, 64, 1), right)

    arrive(got.at[pl.ds(0, NDEV - 1)], send_sem)
    arrive(seven, sum_send)
    arrive(early.at[pl.ds(0, NDEV - 1)], early_send)
    arrive(late.at[pl.ds(0, NDEV - 1)], late_send)
    arrive(result.at[pl.ds(0, NDEV - 1)], final_send)

    for half in range(2):

        @pl.when(tem < NTEM - 1)
        def _():
            downs[half].wait_send()

        @pl.when(tem > 0)
        def _():
            ups[half].wait_send()


def body(across, vertical, template, science, variance, bad_pixels, patch, block):
    vmem = pl.BlockSpec(memory_space=pltpu.VMEM)
    smem = pl.BlockSpec(memory_space=pltpu.SMEM)
    anywhere = pl.BlockSpec(memory_space=pl.ANY)
    dma = pltpu.SemaphoreType.DMA
    return pl.pallas_call(
        kernel,
        out_shape=jax.ShapeDtypeStruct((32, 1024), F32),
        in_specs=[smem, smem] + [anywhere] * 6,
        out_specs=vmem,
        scratch_shapes=[
            pltpu.VMEM(science.shape, BF16),
            pltpu.VMEM(variance.shape, BF16),
            pltpu.VMEM(bad_pixels.shape, jnp.int32),
            pltpu.VMEM(across.shape, BF16),
            pltpu.VMEM(vertical.shape, BF16),
            pltpu.VMEM((18, 16, 128), BF16),
            pltpu.VMEM((NDEV, 18, 16, 128), BF16),
            pltpu.VMEM((1024, 128), F32),
            pltpu.VMEM((NDEV, 16, 128), BF16),
            pltpu.VMEM((NDEV, 12, 128), BF16),
            pltpu.VMEM((NDEV, 16, 128), BF16),
            pltpu.VMEM((NDEV, 12, 128), BF16),
            pltpu.VMEM((2, 2, 12, 16, 256), BF16),
            pltpu.VMEM((2, 2, 12, 16, 256), BF16),
            pltpu.VMEM((SLOTS, 64, 512), BF16),
            pltpu.VMEM((6, 128, 2048), BF16),
            pltpu.VMEM((6, 24, 144), F32),
            pltpu.VMEM((24, 128), F32),
            pltpu.VMEM((NTEM, 24, 128), F32),
            pltpu.VMEM((192, 128), F32),
            pltpu.VMEM((17, 8, 128), F32),
            pltpu.VMEM((128, 128), F32),
            pltpu.VMEM((NDEV, SLOTS, 128), F32),
            pltpu.VMEM((1536, 512), BF16),
            pltpu.VMEM((NDEV, SLOTS, 128), F32),
            pltpu.VMEM((NDEV, 4, 128), BF16),
            pltpu.VMEM((NDEV, 4, 128), BF16),
            dma, dma((5,)), dma, dma((3,)), dma((2, 8, 4)), dma((2, 8)), dma((3, NZ)),
            dma((2, 2)), dma((2, 2)), dma, dma, dma, dma, dma, dma, dma, dma,
        ],
        compiler_params=pltpu.CompilerParams(collective_id=0, has_side_effects=True),
    )(patch.T, block.T, template[0], science, variance, bad_pixels, across, vertical)[None]


def solution(mesh):
    with jax.ensure_compile_time_eval():
        across, vertical = tables()
    across = jnp.asarray(across).astype(BF16)
    vertical = jnp.asarray(vertical).astype(BF16)
    return jax.shard_map(
        functools.partial(body, across, vertical),
        mesh=mesh,
        in_specs=(
            P("visit", "template", None),
            P("visit", None, "template", None),
            P("visit", None, "template", None),
            P("visit", None, "template", None),
            P("visit", None),
            P("visit", None),
        ),
        out_specs=P("visit", "template", None),
        check_vma=False,
    )
```

```python
import functools

import jax
import jax.numpy as jnp
import numpy as np
from jax import lax
from jax.experimental import pallas as pl
from jax.experimental.pallas import tpu as pltpu
from jax.sharding import PartitionSpec as P

NBLK = 8
MARGIN = 64
HALF = 10
RIDGE = 0.05
NZ, NY = 16, 4
NDEV = NZ * NY
NTEM = 8
MESH = pl.DeviceIdType.MESH
F32 = jnp.float32
BF16 = jnp.bfloat16


def basis_taps():
    spread = jnp.arange(2 * HALF + 1, dtype=jnp.float32)
    scaled = (HALF - spread) / 2.5
    hermite = jnp.stack(
        [
            jnp.ones(scaled.shape, jnp.float32),
            2.0 * scaled,
            4.0 * scaled * scaled - 2.0,
            8.0 * scaled * scaled * scaled - 12.0 * scaled,
        ]
    )
    shaped = hermite * jnp.exp(-0.5 * scaled * scaled)
    shaped = shaped / jnp.sqrt(jnp.sum(shaped * shaped, axis=1, keepdims=True))
    return shaped.astype(jnp.bfloat16)


def tables():
    profile = np.asarray(basis_taps().astype(jnp.float32))
    across = np.zeros((256, 4, 128), np.float32)
    vertical = np.zeros((4, 32, 64), np.float32)
    for t in range(2 * HALF + 1):
        for c in range(128):
            across[c + t + MARGIN - HALF, :, c] = profile[:, t]
        for r in range(32):
            vertical[:, r, r + t + 16 - HALF] = profile[:, t]
    return across.reshape(256, 512), vertical.reshape(128, 64)


def wrap(value, size):
    return lax.rem(value + size, size)


TILES = 9
LEAD = 9
SLOTS = 24
HALFWAY = (1, -1)
Y_STEP = {0: 0, 1: 1, 2: 2, 3: -1}


def kernel(
    patch, block, strip, science_in, variance_in, bad_in, across_in, vertical_in, out,
    science, variance, bad, across, vertical,
    stage, got, packed, early, late, early_in, late_in, core, rim, smooth, images,
    sums, part, parts, rows, coef, codes, column, choose, result, final,
    local_sem, input_sem, send_sem, ay, az, bz, by, halo_send, halo_recv, sum_send, sum_recv,
    early_send, early_recv, late_send, late_recv, final_send, final_recv,
):
    me = lax.axis_index("visit")
    tem = lax.axis_index("template")
    z, y = lax.div(me, NY), lax.rem(me, NY)
    visits = science.shape[0]
    inputs = (science, variance, bad, across, vertical)

    def at(dz, dy):
        return (wrap(z + dz, NZ) * NY + wrap(y + dy, NY), tem)

    def beside(step):
        return (me, wrap(tem + step, NTEM))

    def send(src, dst, sem, recv, target):
        copy = pltpu.make_async_remote_copy(
            src_ref=src, dst_ref=dst, send_sem=sem, recv_sem=recv,
            device_id=target, device_id_type=MESH,
        )
        copy.start()
        return copy

    def arrive(ref, sem):
        pltpu.make_async_copy(ref, ref, sem).wait()

    barrier = pltpu.get_barrier_semaphore()
    partners = [at(0, 1), at(0, -1), at(0, 2), at(1, 0), at(-1, 0)]
    partners += [beside(d) for d in range(1, NTEM)]
    for partner in partners:
        pl.semaphore_signal(barrier, inc=1, device_id=partner, device_id_type=MESH)

    for h in range(2):
        for c in range(TILES):
            pltpu.make_async_copy(
                strip.at[pl.ds(16 * h, 16), pl.ds(128 * c, 128)],
                stage.at[h * TILES + c],
                local_sem,
            ).start()

    sources = (science_in, variance_in, bad_in, across_in, vertical_in)
    for k in range(5):
        pltpu.make_async_copy(sources[k], inputs[k], input_sem.at[k]).start()
    arrive(stage, local_sem)
    pl.semaphore_wait(barrier, len(partners))

    def slot(zz, yy):
        return wrap(zz, NZ) * NY + wrap(yy, NY)

    def a_ref(zz, yy):
        return got.at[slot(zz, yy), pl.ds(0, LEAD)]

    def b_ref(zz, yy):
        return got.at[slot(zz, yy), pl.ds(LEAD, 2 * TILES - LEAD)]

    a_own, b_own = stage.at[pl.ds(0, LEAD)], stage.at[pl.ds(LEAD, 2 * TILES - LEAD)]
    for d in (1, 3, 2):
        send(a_own, a_ref(z, y), send_sem, ay.at[d - 1], at(0, Y_STEP[d]))
    for k, dz in enumerate(HALFWAY):
        send(b_own, b_ref(z, y), send_sem, bz.at[k, 0], at(dz, 0))
        send(a_own, a_ref(z, y), send_sem, az.at[k, 0, 0], at(dz, 0))
    for k, dy in enumerate(HALFWAY):
        send(b_own, b_ref(z, y), send_sem, by.at[k, 0], at(0, dy))
    got[me] = stage[...]
    for k in range(5):
        arrive(inputs[k], input_sem.at[k])
    low = lax.broadcasted_iota(jnp.int32, (32, 128), 1) < 64
    lane = lax.broadcasted_iota(jnp.int32, (8, 128), 1)

    def weigh(v, j):
        return (1 - bad[v, j]).astype(F32) / variance[v, j].astype(F32)

    def pack(index, here, there, pitch):
        packed[pl.ds(index, 32, stride=pitch), :] = jnp.where(low, here, pltpu.roll(there, 64, 1))
        packed[pl.ds(32 * pitch + index, 32, stride=pitch), :] = jnp.where(
            low, pltpu.roll(here, 64, 1), there
        )

    targets = jnp.zeros((8, 128), F32)
    for v in range(visits):
        for j in range(4):
            code = (block[j, v] & 1) * 256 + patch[j, v] * 4 + (block[j, v] >> 1) - 256
            code = jnp.full((8, 128), code, jnp.int32).astype(F32)
            targets = jnp.where(lane == v * 4 + j, code, targets)
            if v < visits // 2:
                pack(v * 4 + j, weigh(v, j), weigh(v + 3, j), 16)
    packed[pl.ds(12, NDEV, stride=16), :] = jnp.broadcast_to(targets[0:1], (NDEV, 128))
    early[...] = packed[...].reshape(NDEV, 4, 4, 128).astype(BF16)
    for d in (1, 3, 2):
        ref = a_ref(z, y - Y_STEP[d])
        arrive(ref, ay.at[d - 1])
        for k, dz in enumerate(HALFWAY):
            send(ref, ref, send_sem, az.at[k, 0, d], at(dz, 0))

    def relay(source, index):
        k = index % 2
        dy = HALFWAY[k]
        ref = b_ref(source, y - dy)
        arrive(ref, by.at[k, index])
        send(ref, ref, send_sem, by.at[2, index], at(0, dy))

    ring = NZ // 2

    def z_first(s):
        for k, dz in enumerate(HALFWAY):
            if s == ring and k == 1:
                continue
            ref = b_ref(z - dz * s, y)
            arrive(ref, bz.at[k, s - 1])
            if s < ring - k:
                send(ref, ref, send_sem, bz.at[k, s], at(dz, 0))
            for q, dy in enumerate(HALFWAY):
                send(ref, ref, send_sem, by.at[q, 2 * s - 1 + k], at(0, dy))

    def y_first(s, d):
        for k, dz in enumerate(HALFWAY):
            if s == ring and k != (d >= 2):
                continue
            ref = a_ref(z - dz * s, y - Y_STEP[d])
            arrive(ref, az.at[k, s - 1, d])
            if s < ring - 1 or (s == ring - 1 and k == (d >= 2)):
                send(ref, ref, send_sem, az.at[k, s, d], at(dz, 0))

    def relays(s):
        if s == 0:
            relay(z, 0)
        for k, dz in enumerate(HALFWAY):
            if s > 0 and 2 * s - 1 + k < NZ:
                relay(z - dz * s, 2 * s - 1 + k)

    due = {7 * (s - 1) // 2: s for s in range(1, ring + 1)}
    for index in range(4 * ring):
        if index in due:
            z_first(due[index])
            relays(due[index] - 1)
        if index == 4 * ring - 4:
            relays(ring)
        y_first(index // 4 + 1, (0, 1, 3, 2)[index % 4])
    for index in range(NZ):
        s = (index + 1) // 2
        source = z - s if index % 2 == 1 else z + s
        k = index % 2
        arrive(b_ref(source, y + HALFWAY[k]), by.at[1 - k, index])
        arrive(b_ref(source, y + 2), by.at[2, index])

    def peer(s):
        return lax.rem(me + s, NDEV)

    def push(source, dest, sem, recv):
        def one(s):
            send(source.at[peer(s)], dest.at[me], sem, recv, (peer(s), tem))

        def two(m, carry):
            one(NDEV // 2 - m)
            one(NDEV // 2 + m)
            return carry

        one(NDEV // 2)
        lax.fori_loop(1, NDEV // 2, two, 0)

    def halo(half, source, dest, step, k):
        return pltpu.make_async_remote_copy(
            src_ref=core.at[half, source], dst_ref=rim.at[half, dest],
            send_sem=halo_send.at[half, k], recv_sem=halo_recv.at[half, k],
            device_id=beside(step), device_id_type=MESH,
        )

    downs = [halo(half, 1, 0, 1, 0) for half in range(2)]
    ups = [halo(half, 0, 1, -1, 1) for half in range(2)]
    for half in range(2):
        for v in range(3):
            for j in range(4):
                p, b = patch[j, half * 3 + v], block[j, half * 3 + v]
                for h in range(2):
                    core[half, h, v * 4 + j, :, 0:128] = got[p, h * TILES + b]
                    core[half, h, v * 4 + j, :, 128:256] = got[p, h * TILES + b + 1]

        @pl.when(tem < NTEM - 1)
        def _():
            downs[half].start()

        @pl.when(tem > 0)
        def _():
            ups[half].start()

    def smear(half, piece, source):
        image = jnp.dot(
            source.reshape(12 * 16, 256), across[...], preferred_element_type=F32
        )
        smooth[half * 12 : half * 12 + 12, piece * 16 : piece * 16 + 16, :] = image.astype(
            BF16
        ).reshape(12, 16, 512)

    push(early, early_in, early_send, early_recv)
    early_in[me] = early[me]
    for half in range(2):
        smear(half, 1, core[half, 0])
        smear(half, 2, core[half, 1])

    @pl.when(tem == 0)
    def _():
        rim[:, 0] = jnp.zeros((2, 12, 16, 256), BF16)

    @pl.when(tem == NTEM - 1)
    def _():
        rim[:, 1] = jnp.zeros((2, 12, 16, 256), BF16)

    row_id = lax.broadcasted_iota(jnp.int32, (144, 144), 0) & 7
    lane_id = lax.broadcasted_iota(jnp.int32, (144, 144), 1) & 7
    same_row = row_id == lane_id

    def gram(v, carry):
        ones, extra = [None] * 16, [None] * 16
        for j in range(4):
            image = jnp.dot(vertical[...], smooth[v * 4 + j], preferred_element_type=F32)
            usable = (1 - bad[v, j]).astype(F32)
            masked = usable * science[v, j].astype(F32)
            for g in range(4):
                tile = g * 4 + j
                rows_of = slice(g * 8, g * 8 + 8)
                for a in range(4):
                    pieces = [
                        image[b * 32 + g * 8 : b * 32 + g * 8 + 8, a * 128 : a * 128 + 128]
                        for b in range(4)
                    ]
                    images[v, a * 32 : a * 32 + 32, tile * 128 : tile * 128 + 128] = (
                        jnp.concatenate(pieces, axis=0).astype(BF16)
                    )
                some = usable[rows_of]
                ones[tile] = jnp.concatenate([some, some], axis=0).astype(BF16)
                extra[tile] = jnp.concatenate([some, masked[rows_of]], axis=0).astype(BF16)
        ones = jnp.concatenate(ones, axis=1)
        extra = jnp.concatenate(extra, axis=1)
        left = images[v]
        right = jnp.concatenate([left * jnp.concatenate([ones] * 8, axis=0), extra], axis=0)
        left = jnp.concatenate([left, extra], axis=0)
        full = lax.dot_general(
            left, right, (((1,), (1,)), ((), ())), preferred_element_type=F32
        )
        full = jnp.where(same_row, full, 0.0)
        sums[v, 0:18, :] = jnp.sum(full.reshape(18, 8, 144), axis=1)
        sums[v, 18:24, :] = jnp.zeros((6, 144), F32)
        return carry

    for half in range(2):

        @pl.when(tem > 0)
        def _():
            downs[half].wait_recv()

        @pl.when(tem < NTEM - 1)
        def _():
            ups[half].wait_recv()

        smear(half, 0, rim[half, 0])
        smear(half, 3, rim[half, 1])
        lax.fori_loop(half * 3, half * 3 + 3, gram, 0)
    pick_row = lax.broadcasted_iota(jnp.int32, (144, 128), 0) >> 3
    pick_lane = lax.broadcasted_iota(jnp.int32, (144, 128), 1)
    dense = jnp.dot(
        sums[...].reshape(144, 144), (pick_lane == pick_row).astype(F32),
        preferred_element_type=F32, precision=lax.Precision.HIGHEST,
    )
    mine = dense[0:24]
    for v in range(1, visits):
        mine = mine + pltpu.roll(dense[v * 24 : v * 24 + 24], 20 * v, 1)
    part[...] = mine
    for d in range(1, NTEM):
        send(part, parts.at[tem], sum_send, sum_recv, beside(d))
    parts[tem] = part[...]
    seven = parts.at[pl.ds(0, NTEM - 1)]
    arrive(seven, sum_recv)
    total = parts[0]
    for d in range(1, NTEM):
        total = total + parts[d]

    rows[...] = jnp.zeros((192, 128), F32)
    for v in range(visits):
        moved = total if v == 0 else pltpu.roll(total, 128 - 20 * v, 1)
        rows[pl.ds(v, 24, stride=8), :] = moved
    system = [rows[k * 8 : k * 8 + 8, :] for k in range(17)]
    ridge = RIDGE * (system[16][:, 16:17] + 1.0)
    system = [jnp.where(lane == k, system[k] + ridge, system[k]) for k in range(17)]
    for c in range(17):
        pivot = system[c] / system[c][:, c : c + 1]
        system = [
            pivot if k == c else system[k] - system[k][:, c : c + 1] * pivot for k in range(17)
        ]
    for k in range(17):
        coef[k] = jnp.broadcast_to(system[k][:, 17:18], (8, 128))

    def differ(v, carry):
        numbers = []
        for w in (v, v + 3):
            factors = [jnp.broadcast_to(coef[k, pl.ds(w, 1), :], (8, 128)) for k in range(17)]
            for j in range(4):
                models = []
                for g in range(4):
                    tile = g * 4 + j
                    model = factors[16]
                    for a in range(4):
                        image = images[
                            w, a * 32 : a * 32 + 32, tile * 128 : tile * 128 + 128
                        ].astype(F32)
                        for b in range(4):
                            model = model + factors[a * 4 + b] * image[b * 8 : b * 8 + 8]
                    models.append(model)
                model = jnp.concatenate(models, axis=0)
                numbers.append(weigh(w, j) * (science[w, j].astype(F32) - model))
        for j in range(4):
            pack(v * 4 + j, numbers[j], numbers[4 + j], 12)
        return carry

    lax.fori_loop(0, visits // 2, differ, 0)
    late[...] = packed[0:768, :].reshape(NDEV, 3, 4, 128).astype(BF16)
    push(late, late_in, late_send, late_recv)
    late_in[me] = late[me]

    arrive(early_in.at[pl.ds(0, NDEV - 1)], early_recv)
    codes[...] = jnp.zeros((128, 128), F32)
    for k in range(NDEV):
        codes[k : k + 1, :] = early_in[k, 3].astype(F32)[0:1]
    across_codes = codes[...].T
    place = lax.broadcasted_iota(jnp.int32, (NDEV * 12, 128), 1).astype(F32)
    for p in range(2):
        for k in range(NDEV):
            column[p, k * 12 : k * 12 + 12, :] = jnp.broadcast_to(
                across_codes[p * 12 : p * 12 + 12, k : k + 1], (12, 128)
            )
        code = column[p]
        for q in range(4):
            choose[p, :, q * 128 : q * 128 + 128] = jnp.where(
                code == place + (q * 128.0 - 256.0), 1.0, 0.0
            ).astype(BF16)

    def collect(box):
        values = box.astype(F32).reshape(NDEV * 12, 128).astype(BF16)
        inner = (((0,), (0,)), ((), ()))
        sums = [
            lax.dot_general(values, choose[p], inner, preferred_element_type=F32)
            for p in range(2)
        ]
        return sums[0][0:64] + sums[1][64:128]

    denominator = collect(early_in[:, 0:3])
    scale = jnp.sqrt(jnp.maximum(denominator, 1.0))

    arrive(late_in.at[pl.ds(0, NDEV - 1)], late_recv)
    numerator = collect(late_in[...])
    ratio = numerator / scale
    both = jnp.concatenate([ratio[:, 0:256], ratio[:, 256:512]], axis=0).T
    result[...] = both.reshape(NDEV, 4, 128)
    push(result, final, final_send, final_recv)
    final[me] = result[me]
    arrive(final.at[pl.ds(0, NDEV - 1)], final_recv)
    whole = final[...]
    for m in range(4):
        left, right = whole[0:32, m, :], whole[32:64, m, :]
        out[:, m * 256 : m * 256 + 128] = jnp.where(low, left, pltpu.roll(right, 64, 1))
        out[:, m * 256 + 128 : m * 256 + 256] = jnp.where(low, pltpu.roll(left, 64, 1), right)

    arrive(got.at[pl.ds(0, NDEV - 1)], send_sem)
    arrive(seven, sum_send)
    arrive(early.at[pl.ds(0, NDEV - 1)], early_send)
    arrive(late.at[pl.ds(0, NDEV - 1)], late_send)
    arrive(result.at[pl.ds(0, NDEV - 1)], final_send)

    for half in range(2):

        @pl.when(tem < NTEM - 1)
        def _():
            downs[half].wait_send()

        @pl.when(tem > 0)
        def _():
            ups[half].wait_send()


def body(across, vertical, template, science, variance, bad_pixels, patch, block):
    vmem = pl.BlockSpec(memory_space=pltpu.VMEM)
    smem = pl.BlockSpec(memory_space=pltpu.SMEM)
    anywhere = pl.BlockSpec(memory_space=pl.ANY)
    dma = pltpu.SemaphoreType.DMA
    return pl.pallas_call(
        kernel,
        out_shape=jax.ShapeDtypeStruct((32, 1024), F32),
        in_specs=[smem, smem] + [anywhere] * 6,
        out_specs=vmem,
        scratch_shapes=[
            pltpu.VMEM(science.shape, BF16),
            pltpu.VMEM(variance.shape, BF16),
            pltpu.VMEM(bad_pixels.shape, jnp.int32),
            pltpu.VMEM(across.shape, BF16),
            pltpu.VMEM(vertical.shape, BF16),
            pltpu.VMEM((18, 16, 128), BF16),
            pltpu.VMEM((NDEV, 18, 16, 128), BF16),
            pltpu.VMEM((1024, 128), F32),
            pltpu.VMEM((NDEV, 4, 4, 128), BF16),
            pltpu.VMEM((NDEV, 3, 4, 128), BF16),
            pltpu.VMEM((NDEV, 4, 4, 128), BF16),
            pltpu.VMEM((NDEV, 3, 4, 128), BF16),
            pltpu.VMEM((2, 2, 12, 16, 256), BF16),
            pltpu.VMEM((2, 2, 12, 16, 256), BF16),
            pltpu.VMEM((SLOTS, 64, 512), BF16),
            pltpu.VMEM((6, 128, 2048), BF16),
            pltpu.VMEM((6, 24, 144), F32),
            pltpu.VMEM((24, 128), F32),
            pltpu.VMEM((NTEM, 24, 128), F32),
            pltpu.VMEM((192, 128), F32),
            pltpu.VMEM((17, 8, 128), F32),
            pltpu.VMEM((128, 128), F32),
            pltpu.VMEM((2, NDEV * 12, 128), F32),
            pltpu.VMEM((2, NDEV * 12, 512), BF16),
            pltpu.VMEM((NDEV, 4, 128), F32),
            pltpu.VMEM((NDEV, 4, 128), F32),
            dma, dma((5,)), dma, dma((3,)), dma((2, 8, 4)), dma((2, 8)), dma((3, NZ)),
            dma((2, 2)), dma((2, 2)), dma, dma, dma, dma, dma, dma, dma, dma,
        ],
        compiler_params=pltpu.CompilerParams(collective_id=0, has_side_effects=True),
    )(patch.T, block.T, template[0], science, variance, bad_pixels, across, vertical)[None]


def solution(mesh):
    with jax.ensure_compile_time_eval():
        across, vertical = tables()
    across = jnp.asarray(across).astype(BF16)
    vertical = jnp.asarray(vertical).astype(BF16)
    return jax.shard_map(
        functools.partial(body, across, vertical),
        mesh=mesh,
        in_specs=(
            P("visit", "template", None),
            P("visit", None, "template", None),
            P("visit", None, "template", None),
            P("visit", None, "template", None),
            P("visit", None),
            P("visit", None),
        ),
        out_specs=P("visit", "template", None),
        check_vma=False,
    )
```

```python
import functools

import jax
import jax.numpy as jnp
import numpy as np
from jax import lax
from jax.experimental import pallas as pl
from jax.experimental.pallas import tpu as pltpu
from jax.sharding import PartitionSpec as P

NBLK = 8
MARGIN = 64
HALF = 10
RIDGE = 0.05
NZ, NY = 16, 4
NDEV = NZ * NY
NTEM = 8
MESH = pl.DeviceIdType.MESH
F32 = jnp.float32
BF16 = jnp.bfloat16


def basis_taps():
    spread = jnp.arange(2 * HALF + 1, dtype=jnp.float32)
    scaled = (HALF - spread) / 2.5
    hermite = jnp.stack(
        [
            jnp.ones(scaled.shape, jnp.float32),
            2.0 * scaled,
            4.0 * scaled * scaled - 2.0,
            8.0 * scaled * scaled * scaled - 12.0 * scaled,
        ]
    )
    shaped = hermite * jnp.exp(-0.5 * scaled * scaled)
    shaped = shaped / jnp.sqrt(jnp.sum(shaped * shaped, axis=1, keepdims=True))
    return shaped.astype(jnp.bfloat16)


def tables():
    profile = np.asarray(basis_taps().astype(jnp.float32))
    across = np.zeros((256, 4, 128), np.float32)
    vertical = np.zeros((4, 32, 64), np.float32)
    for t in range(2 * HALF + 1):
        for c in range(128):
            across[c + t + MARGIN - HALF, :, c] = profile[:, t]
        for r in range(32):
            vertical[:, r, r + t + 16 - HALF] = profile[:, t]
    return across.reshape(256, 512), vertical.reshape(128, 64)


def wrap(value, size):
    return lax.rem(value + size, size)


TILES = 9
LEAD = 9
SLOTS = 24
HALFWAY = (1, -1)
Y_STEP = {0: 0, 1: 1, 2: 2, 3: -1}


def kernel(
    patch, block, strip, science_in, variance_in, bad_in, across_in, vertical_in, out,
    science, variance, bad, across, vertical,
    stage, got, packed, early, late, early_in, late_in, core, rim, smooth, images,
    sums, part, parts, rows, coef, codes, column, choose, result, final,
    local_sem, input_sem, send_sem, ay, az, bz, by, halo_send, halo_recv, sum_send, sum_recv,
    early_send, early_recv, late_send, late_recv, final_send, final_recv,
):
    me = lax.axis_index("visit")
    tem = lax.axis_index("template")
    z, y = lax.div(me, NY), lax.rem(me, NY)
    visits = science.shape[0]
    inputs = (science, variance, bad, across, vertical)

    def at(dz, dy):
        return (wrap(z + dz, NZ) * NY + wrap(y + dy, NY), tem)

    def beside(step):
        return (me, wrap(tem + step, NTEM))

    def send(src, dst, sem, recv, target):
        copy = pltpu.make_async_remote_copy(
            src_ref=src, dst_ref=dst, send_sem=sem, recv_sem=recv,
            device_id=target, device_id_type=MESH,
        )
        copy.start()
        return copy

    def arrive(ref, sem):
        pltpu.make_async_copy(ref, ref, sem).wait()

    barrier = pltpu.get_barrier_semaphore()
    partners = [at(0, 1), at(0, -1), at(0, 2), at(1, 0), at(-1, 0)]
    partners += [beside(d) for d in range(1, NTEM)]
    for partner in partners:
        pl.semaphore_signal(barrier, inc=1, device_id=partner, device_id_type=MESH)

    for h in range(2):
        for c in range(TILES):
            pltpu.make_async_copy(
                strip.at[pl.ds(16 * h, 16), pl.ds(128 * c, 128)],
                stage.at[h * TILES + c],
                local_sem,
            ).start()

    sources = (science_in, variance_in, bad_in, across_in, vertical_in)
    for k in range(5):
        pltpu.make_async_copy(sources[k], inputs[k], input_sem.at[k]).start()
    arrive(stage, local_sem)
    pl.semaphore_wait(barrier, len(partners))

    def slot(zz, yy):
        return wrap(zz, NZ) * NY + wrap(yy, NY)

    def a_ref(zz, yy):
        return got.at[slot(zz, yy), pl.ds(0, LEAD)]

    def b_ref(zz, yy):
        return got.at[slot(zz, yy), pl.ds(LEAD, 2 * TILES - LEAD)]

    a_own, b_own = stage.at[pl.ds(0, LEAD)], stage.at[pl.ds(LEAD, 2 * TILES - LEAD)]
    for d in (1, 3, 2):
        send(a_own, a_ref(z, y), send_sem, ay.at[d - 1], at(0, Y_STEP[d]))
    for k, dz in enumerate(HALFWAY):
        send(b_own, b_ref(z, y), send_sem, bz.at[k, 0], at(dz, 0))
        send(a_own, a_ref(z, y), send_sem, az.at[k, 0, 0], at(dz, 0))
    for k, dy in enumerate(HALFWAY):
        send(b_own, b_ref(z, y), send_sem, by.at[k, 0], at(0, dy))
    got[me] = stage[...]
    for d in (1, 3, 2):
        ref = a_ref(z, y - Y_STEP[d])
        arrive(ref, ay.at[d - 1])
        for k, dz in enumerate(HALFWAY):
            send(ref, ref, send_sem, az.at[k, 0, d], at(dz, 0))

    def relay(source, index):
        k = index % 2
        dy = HALFWAY[k]
        ref = b_ref(source, y - dy)
        arrive(ref, by.at[k, index])
        send(ref, ref, send_sem, by.at[2, index], at(0, dy))

    ring = NZ // 2

    def z_first(s):
        for k, dz in enumerate(HALFWAY):
            if s == ring and k == 1:
                continue
            ref = b_ref(z - dz * s, y)
            arrive(ref, bz.at[k, s - 1])
            if s < ring - k:
                send(ref, ref, send_sem, bz.at[k, s], at(dz, 0))
            for q, dy in enumerate(HALFWAY):
                send(ref, ref, send_sem, by.at[q, 2 * s - 1 + k], at(0, dy))

    def y_first(s, d):
        for k, dz in enumerate(HALFWAY):
            if s == ring and k != (d >= 2):
                continue
            ref = a_ref(z - dz * s, y - Y_STEP[d])
            arrive(ref, az.at[k, s - 1, d])
            if s < ring - 1 or (s == ring - 1 and k == (d >= 2)):
                send(ref, ref, send_sem, az.at[k, s, d], at(dz, 0))

    def relays(s):
        if s == 0:
            relay(z, 0)
        for k, dz in enumerate(HALFWAY):
            if s > 0 and 2 * s - 1 + k < NZ:
                relay(z - dz * s, 2 * s - 1 + k)

    due = {7 * (s - 1) // 2: s for s in range(1, ring + 1)}
    for index in range(4 * ring - 4):
        if index in due:
            z_first(due[index])
            relays(due[index] - 1)
        y_first(index // 4 + 1, (0, 1, 3, 2)[index % 4])
    relays(ring)

    for k in range(5):
        arrive(inputs[k], input_sem.at[k])
    low = lax.broadcasted_iota(jnp.int32, (32, 128), 1) < 64
    lane = lax.broadcasted_iota(jnp.int32, (8, 128), 1)

    def weigh(v, j):
        return (1 - bad[v, j]).astype(F32) / variance[v, j].astype(F32)

    def pack(index, here, there, pitch):
        packed[pl.ds(index, 32, stride=pitch), :] = jnp.where(low, here, pltpu.roll(there, 64, 1))
        packed[pl.ds(32 * pitch + index, 32, stride=pitch), :] = jnp.where(
            low, pltpu.roll(here, 64, 1), there
        )

    targets = jnp.zeros((8, 128), F32)
    for v in range(visits):
        for j in range(4):
            code = (block[j, v] & 1) * 256 + patch[j, v] * 4 + (block[j, v] >> 1) - 256
            code = jnp.full((8, 128), code, jnp.int32).astype(F32)
            targets = jnp.where(lane == v * 4 + j, code, targets)
            if v < visits // 2:
                pack(v * 4 + j, weigh(v, j), weigh(v + 3, j), 16)
    packed[pl.ds(12, NDEV, stride=16), :] = jnp.broadcast_to(targets[0:1], (NDEV, 128))
    early[...] = packed[...].reshape(NDEV, 4, 4, 128).astype(BF16)

    for d in (0, 1, 3, 2):
        y_first(ring, d)
    for index in range(NZ):
        s = (index + 1) // 2
        source = z - s if index % 2 == 1 else z + s
        k = index % 2
        arrive(b_ref(source, y + HALFWAY[k]), by.at[1 - k, index])
        arrive(b_ref(source, y + 2), by.at[2, index])

    def peer(s):
        return lax.rem(me + s, NDEV)

    def push(source, dest, sem, recv):
        def one(s):
            send(source.at[peer(s)], dest.at[me], sem, recv, (peer(s), tem))

        def two(m, carry):
            one(NDEV // 2 - m)
            one(NDEV // 2 + m)
            return carry

        one(NDEV // 2)
        lax.fori_loop(1, NDEV // 2, two, 0)

    def halo(half, source, dest, step, k):
        return pltpu.make_async_remote_copy(
            src_ref=core.at[half, source], dst_ref=rim.at[half, dest],
            send_sem=halo_send.at[half, k], recv_sem=halo_recv.at[half, k],
            device_id=beside(step), device_id_type=MESH,
        )

    downs = [halo(half, 1, 0, 1, 0) for half in range(2)]
    ups = [halo(half, 0, 1, -1, 1) for half in range(2)]
    for half in range(2):
        for v in range(3):
            for j in range(4):
                p, b = patch[j, half * 3 + v], block[j, half * 3 + v]
                for h in range(2):
                    core[half, h, v * 4 + j, :, 0:128] = got[p, h * TILES + b]
                    core[half, h, v * 4 + j, :, 128:256] = got[p, h * TILES + b + 1]

        @pl.when(tem < NTEM - 1)
        def _():
            downs[half].start()

        @pl.when(tem > 0)
        def _():
            ups[half].start()

    def smear(half, piece, source):
        image = jnp.dot(
            source.reshape(12 * 16, 256), across[...], preferred_element_type=F32
        )
        smooth[half * 12 : half * 12 + 12, piece * 16 : piece * 16 + 16, :] = image.astype(
            BF16
        ).reshape(12, 16, 512)

    push(early, early_in, early_send, early_recv)
    early_in[me] = early[me]
    for half in range(2):
        smear(half, 1, core[half, 0])
        smear(half, 2, core[half, 1])

    @pl.when(tem == 0)
    def _():
        rim[:, 0] = jnp.zeros((2, 12, 16, 256), BF16)

    @pl.when(tem == NTEM - 1)
    def _():
        rim[:, 1] = jnp.zeros((2, 12, 16, 256), BF16)

    row_id = lax.broadcasted_iota(jnp.int32, (144, 144), 0) & 7
    lane_id = lax.broadcasted_iota(jnp.int32, (144, 144), 1) & 7
    same_row = row_id == lane_id

    def gram(v, carry):
        ones, extra = [None] * 16, [None] * 16
        for j in range(4):
            image = jnp.dot(vertical[...], smooth[v * 4 + j], preferred_element_type=F32)
            usable = (1 - bad[v, j]).astype(F32)
            masked = usable * science[v, j].astype(F32)
            for g in range(4):
                tile = g * 4 + j
                rows_of = slice(g * 8, g * 8 + 8)
                for a in range(4):
                    pieces = [
                        image[b * 32 + g * 8 : b * 32 + g * 8 + 8, a * 128 : a * 128 + 128]
                        for b in range(4)
                    ]
                    images[v, a * 32 : a * 32 + 32, tile * 128 : tile * 128 + 128] = (
                        jnp.concatenate(pieces, axis=0).astype(BF16)
                    )
                some = usable[rows_of]
                ones[tile] = jnp.concatenate([some, some], axis=0).astype(BF16)
                extra[tile] = jnp.concatenate([some, masked[rows_of]], axis=0).astype(BF16)
        ones = jnp.concatenate(ones, axis=1)
        extra = jnp.concatenate(extra, axis=1)
        left = images[v]
        right = jnp.concatenate([left * jnp.concatenate([ones] * 8, axis=0), extra], axis=0)
        left = jnp.concatenate([left, extra], axis=0)
        full = lax.dot_general(
            left, right, (((1,), (1,)), ((), ())), preferred_element_type=F32
        )
        full = jnp.where(same_row, full, 0.0)
        sums[v, 0:18, :] = jnp.sum(full.reshape(18, 8, 144), axis=1)
        sums[v, 18:24, :] = jnp.zeros((6, 144), F32)
        return carry

    for half in range(2):

        @pl.when(tem > 0)
        def _():
            downs[half].wait_recv()

        @pl.when(tem < NTEM - 1)
        def _():
            ups[half].wait_recv()

        smear(half, 0, rim[half, 0])
        smear(half, 3, rim[half, 1])
        lax.fori_loop(half * 3, half * 3 + 3, gram, 0)
    pick_row = lax.broadcasted_iota(jnp.int32, (144, 128), 0) >> 3
    pick_lane = lax.broadcasted_iota(jnp.int32, (144, 128), 1)
    dense = jnp.dot(
        sums[...].reshape(144, 144), (pick_lane == pick_row).astype(F32),
        preferred_element_type=F32, precision=lax.Precision.HIGHEST,
    )
    mine = dense[0:24]
    for v in range(1, visits):
        mine = mine + pltpu.roll(dense[v * 24 : v * 24 + 24], 20 * v, 1)
    part[...] = mine
    for d in range(1, NTEM):
        send(part, parts.at[tem], sum_send, sum_recv, beside(d))
    parts[tem] = part[...]
    seven = parts.at[pl.ds(0, NTEM - 1)]
    arrive(seven, sum_recv)
    total = parts[0]
    for d in range(1, NTEM):
        total = total + parts[d]

    rows[...] = jnp.zeros((192, 128), F32)
    for v in range(visits):
        moved = total if v == 0 else pltpu.roll(total, 128 - 20 * v, 1)
        rows[pl.ds(v, 24, stride=8), :] = moved
    system = [rows[k * 8 : k * 8 + 8, :] for k in range(17)]
    ridge = RIDGE * (system[16][:, 16:17] + 1.0)
    system = [jnp.where(lane == k, system[k] + ridge, system[k]) for k in range(17)]
    for c in range(17):
        pivot = system[c] / system[c][:, c : c + 1]
        system = [
            pivot if k == c else system[k] - system[k][:, c : c + 1] * pivot for k in range(17)
        ]
    for k in range(17):
        coef[k] = jnp.broadcast_to(system[k][:, 17:18], (8, 128))

    def differ(v, carry):
        numbers = []
        for w in (v, v + 3):
            factors = [jnp.broadcast_to(coef[k, pl.ds(w, 1), :], (8, 128)) for k in range(17)]
            for j in range(4):
                models = []
                for g in range(4):
                    tile = g * 4 + j
                    model = factors[16]
                    for a in range(4):
                        image = images[
                            w, a * 32 : a * 32 + 32, tile * 128 : tile * 128 + 128
                        ].astype(F32)
                        for b in range(4):
                            model = model + factors[a * 4 + b] * image[b * 8 : b * 8 + 8]
                    models.append(model)
                model = jnp.concatenate(models, axis=0)
                numbers.append(weigh(w, j) * (science[w, j].astype(F32) - model))
        for j in range(4):
            pack(v * 4 + j, numbers[j], numbers[4 + j], 12)
        return carry

    lax.fori_loop(0, visits // 2, differ, 0)
    late[...] = packed[0:768, :].reshape(NDEV, 3, 4, 128).astype(BF16)
    push(late, late_in, late_send, late_recv)
    late_in[me] = late[me]

    arrive(early_in.at[pl.ds(0, NDEV - 1)], early_recv)
    codes[...] = jnp.zeros((128, 128), F32)
    for k in range(NDEV):
        codes[k : k + 1, :] = early_in[k, 3].astype(F32)[0:1]
    across_codes = codes[...].T
    place = lax.broadcasted_iota(jnp.int32, (NDEV * 12, 128), 1).astype(F32)
    for p in range(2):
        for k in range(NDEV):
            column[p, k * 12 : k * 12 + 12, :] = jnp.broadcast_to(
                across_codes[p * 12 : p * 12 + 12, k : k + 1], (12, 128)
            )
        code = column[p]
        for q in range(4):
            choose[p, :, q * 128 : q * 128 + 128] = jnp.where(
                code == place + (q * 128.0 - 256.0), 1.0, 0.0
            ).astype(BF16)

    def collect(box):
        values = box.astype(F32).reshape(NDEV * 12, 128).astype(BF16)
        inner = (((0,), (0,)), ((), ()))
        sums = [
            lax.dot_general(values, choose[p], inner, preferred_element_type=F32)
            for p in range(2)
        ]
        return sums[0][0:64] + sums[1][64:128]

    denominator = collect(early_in[:, 0:3])
    scale = jnp.sqrt(jnp.maximum(denominator, 1.0))

    arrive(late_in.at[pl.ds(0, NDEV - 1)], late_recv)
    numerator = collect(late_in[...])
    ratio = numerator / scale
    both = jnp.concatenate([ratio[:, 0:256], ratio[:, 256:512]], axis=0).T
    result[...] = both.reshape(NDEV, 4, 128)
    push(result, final, final_send, final_recv)
    final[me] = result[me]
    arrive(final.at[pl.ds(0, NDEV - 1)], final_recv)
    whole = final[...]
    for m in range(4):
        left, right = whole[0:32, m, :], whole[32:64, m, :]
        out[:, m * 256 : m * 256 + 128] = jnp.where(low, left, pltpu.roll(right, 64, 1))
        out[:, m * 256 + 128 : m * 256 + 256] = jnp.where(low, pltpu.roll(left, 64, 1), right)

    arrive(got.at[pl.ds(0, NDEV - 1)], send_sem)
    arrive(seven, sum_send)
    arrive(early.at[pl.ds(0, NDEV - 1)], early_send)
    arrive(late.at[pl.ds(0, NDEV - 1)], late_send)
    arrive(result.at[pl.ds(0, NDEV - 1)], final_send)

    for half in range(2):

        @pl.when(tem < NTEM - 1)
        def _():
            downs[half].wait_send()

        @pl.when(tem > 0)
        def _():
            ups[half].wait_send()


def body(across, vertical, template, science, variance, bad_pixels, patch, block):
    vmem = pl.BlockSpec(memory_space=pltpu.VMEM)
    smem = pl.BlockSpec(memory_space=pltpu.SMEM)
    anywhere = pl.BlockSpec(memory_space=pl.ANY)
    dma = pltpu.SemaphoreType.DMA
    return pl.pallas_call(
        kernel,
        out_shape=jax.ShapeDtypeStruct((32, 1024), F32),
        in_specs=[smem, smem] + [anywhere] * 6,
        out_specs=vmem,
        scratch_shapes=[
            pltpu.VMEM(science.shape, BF16),
            pltpu.VMEM(variance.shape, BF16),
            pltpu.VMEM(bad_pixels.shape, jnp.int32),
            pltpu.VMEM(across.shape, BF16),
            pltpu.VMEM(vertical.shape, BF16),
            pltpu.VMEM((18, 16, 128), BF16),
            pltpu.VMEM((NDEV, 18, 16, 128), BF16),
            pltpu.VMEM((1024, 128), F32),
            pltpu.VMEM((NDEV, 4, 4, 128), BF16),
            pltpu.VMEM((NDEV, 3, 4, 128), BF16),
            pltpu.VMEM((NDEV, 4, 4, 128), BF16),
            pltpu.VMEM((NDEV, 3, 4, 128), BF16),
            pltpu.VMEM((2, 2, 12, 16, 256), BF16),
            pltpu.VMEM((2, 2, 12, 16, 256), BF16),
            pltpu.VMEM((SLOTS, 64, 512), BF16),
            pltpu.VMEM((6, 128, 2048), BF16),
            pltpu.VMEM((6, 24, 144), F32),
            pltpu.VMEM((24, 128), F32),
            pltpu.VMEM((NTEM, 24, 128), F32),
            pltpu.VMEM((192, 128), F32),
            pltpu.VMEM((17, 8, 128), F32),
            pltpu.VMEM((128, 128), F32),
            pltpu.VMEM((2, NDEV * 12, 128), F32),
            pltpu.VMEM((2, NDEV * 12, 512), BF16),
            pltpu.VMEM((NDEV, 4, 128), F32),
            pltpu.VMEM((NDEV, 4, 128), F32),
            dma, dma((5,)), dma, dma((3,)), dma((2, 8, 4)), dma((2, 8)), dma((3, NZ)),
            dma((2, 2)), dma((2, 2)), dma, dma, dma, dma, dma, dma, dma, dma,
        ],
        compiler_params=pltpu.CompilerParams(collective_id=0, has_side_effects=True),
    )(patch.T, block.T, template[0], science, variance, bad_pixels, across, vertical)[None]


def solution(mesh):
    with jax.ensure_compile_time_eval():
        across, vertical = tables()
    across = jnp.asarray(across).astype(BF16)
    vertical = jnp.asarray(vertical).astype(BF16)
    return jax.shard_map(
        functools.partial(body, across, vertical),
        mesh=mesh,
        in_specs=(
            P("visit", "template", None),
            P("visit", None, "template", None),
            P("visit", None, "template", None),
            P("visit", None, "template", None),
            P("visit", None),
            P("visit", None),
        ),
        out_specs=P("visit", "template", None),
        check_vma=False,
    )
```
